32 devices in a mesh: dp: 8 (over z, y), tensor: 4 (over x, core).
Axes of the slice: x: 2, y: 2, z: 4, core: 2. Of those that a mesh axis runs over, the one named last changes fastest.
Arguments:
- hidden_in: bfloat16 [4096, 768], P('dp'), may hold values from -6 to 6
- out_cotangent: bfloat16 [4096, 768], P('dp'), may hold values from -6 to 6
- class_label: int32 [16], replicated, may hold values from 0 to 1000
- time_step: int32 [16], replicated, may hold values from 0 to 999
- modulation_weight: bfloat16 [768, 4608], P(None, 'tensor'), may hold values from -0.21875 to 0.21875
- modulation_bias: bfloat16 [4608], P('tensor'), may hold values from -3 to 3
- heads_weight: bfloat16 [768, 3, 768], P(None, None, 'tensor'), may hold values from -0.15625 to 0.15625
- heads_bias: bfloat16 [2, 768], P(None, 'tensor'), may hold values from -3 to 3
- mixing_weight: bfloat16 [768, 768], P('tensor'), may hold values from -1.25 to 1.25
- mixing_bias: bfloat16 [768], replicated, may hold values from -3 to 3
- up_weight: bfloat16 [768, 3072], P(None, 'tensor'), may hold values from -0.15625 to 0.15625
- up_bias: bfloat16 [3072], P('tensor'), may hold values from -3 to 3
- down_weight: bfloat16 [3072, 768], P('tensor'), may hold values from -0.109375 to 0.109375
- down_bias: bfloat16 [768], replicated, may hold values from -3 to 3
- class_table: bfloat16 [1001, 768], P(None, 'tensor'), may hold values from -6 to 6
- time_table: bfloat16 [1000, 768], P(None, 'tensor'), may hold values from -6 to 6
Outputs:
- block_out: bfloat16 [4096, 768], P('dp')
- input_grad: float32 [4096, 768], P('dp')
- modulation_weight_grad: float32 [768, 4608], P(None, 'tensor')
- modulation_bias_grad: float32 [4608], P('tensor')
- heads_weight_grad: float32 [768, 3, 768], P(None, None, 'tensor')
- heads_bias_grad: float32 [2, 768], P(None, 'tensor')
- mixing_weight_grad: float32 [768, 768], P('tensor')
- mixing_bias_grad: float32 [768], replicated
- up_weight_grad: float32 [768, 3072], P(None, 'tensor')
- up_bias_grad: float32 [3072], P('tensor')
- down_weight_grad: float32 [3072, 768], P('tensor')
- down_bias_grad: float32 [768], replicated
- class_table_grad: float32 [1001, 768], P(None, 'tensor')
- time_table_grad: float32 [1000, 768], P(None, 'tensor')
The draws below stay inside these ranges and needn't reach their ends.
All inputs are finite; a program needn't handle non-finite values.
Results may differ from the reference program's by a relative error of at most 0.023.
Values sent between devices are 32-bit elements; how exact they have to be, the bound alone decides.
No kernel may reach another device: no remote copies, remote signals or barrier semaphores. Data moves between devices by JAX's collectives and lax.ppermute only.
A program may use at most 128 MiB of HBM per device.

```python
import math
import jax
import jax.numpy as jnp
from jax import lax

D = 768
HEADS = 12
FF = 3072
SEQ = 256
NCLASS = 1001
NSTEPS = 1000
HEAD_DIM = 64
LATENTS = 16
TOKENS = 4096


def set_ends(drawn, stream_key, least, top_value):
    shape = drawn.shape
    place = [jax.random.randint(jax.random.fold_in(stream_key, axis), (), 0, shape[axis]) for axis in range(len(shape))]
    drawn = drawn.at[tuple(place)].set(least)
    longest = shape.index(max(shape))
    place[longest] = (place[longest] + 1) % shape[longest]
    return drawn.at[tuple(place)].set(top_value)


def steps_of(key, extent, split, least, largest):
    loudness = 1.0
    for axis_at, shards_of in split:
        steps = jax.random.uniform(jax.random.fold_in(jax.random.fold_in(key, 6), axis_at), (shards_of,), jnp.float32, least / len(split), largest / len(split))
        loudness = loudness * jnp.repeat(jnp.exp(steps), extent[axis_at] // shards_of).reshape((-1,) + (1,) * (len(extent) - 1 - axis_at))
    return loudness


def normal_values(stream_key, dims, deviation, limit, split=(), dtype=jnp.bfloat16):
    level = steps_of(stream_key, dims, split, -0.22, 0.18) if split else 1.0
    values = jax.random.normal(stream_key, dims, jnp.float32) * deviation * level
    return jnp.minimum(jnp.maximum(values, -limit), limit).astype(dtype)


def setup_inputs(seed: int = 0) -> dict:
    arg_keys = jax.random.split(jax.random.key(seed), 17)
    hidden_in = normal_values(arg_keys[0], (TOKENS, D), 1.0, 6.0, ((0, 8),))
    out_cotangent = normal_values(arg_keys[1], (TOKENS, D), 1.0, 6.0, ((0, 8),))
    class_label = set_ends(jax.random.randint(arg_keys[2], (LATENTS,), 0, NCLASS), jax.random.fold_in(arg_keys[2], 1), 0, NCLASS - 1).astype(jnp.int32)
    time_step = set_ends(jax.random.randint(arg_keys[3], (LATENTS,), 0, NSTEPS), jax.random.fold_in(arg_keys[3], 1), 0, NSTEPS - 1).astype(jnp.int32)
    modulation_weight = normal_values(arg_keys[4], (D, 6 * D), D ** -0.5, 0.21875, ((1, 4),))
    modulation_bias = normal_values(arg_keys[5], (6 * D,), 0.5, 3.0, ((0, 4),))
    heads_weight = normal_values(arg_keys[6], (D, 3, D), (2 * D) ** -0.5, 0.15625, ((2, 4),))
    heads_bias = normal_values(arg_keys[7], (2, D), 0.5, 3.0, ((1, 4),))
    mixing_weight = normal_values(arg_keys[8], (D, D), (D // 32) ** -0.5, 1.25, ((0, 4),))
    mixing_bias = normal_values(arg_keys[9], (D,), 0.5, 3.0)
    up_weight = normal_values(arg_keys[10], (D, FF), (2 * D) ** -0.5, 0.15625, ((1, 4),))
    up_bias = normal_values(arg_keys[11], (FF,), 0.5, 3.0, ((0, 4),))
    down_weight = normal_values(arg_keys[12], (FF, D), FF ** -0.5, 0.109375, ((0, 4),))
    down_bias = normal_values(arg_keys[13], (D,), 0.5, 3.0)
    class_table = normal_values(arg_keys[14], (NCLASS, D), 1.0, 6.0, ((1, 4),))
    time_table = normal_values(arg_keys[15], (NSTEPS, D), 1.0, 6.0, ((1, 4),))
    return dict(hidden_in=hidden_in, out_cotangent=out_cotangent, class_label=class_label, time_step=time_step, modulation_weight=modulation_weight, modulation_bias=modulation_bias, heads_weight=heads_weight, heads_bias=heads_bias, mixing_weight=mixing_weight, mixing_bias=mixing_bias, up_weight=up_weight, up_bias=up_bias, down_weight=down_weight, down_bias=down_bias, class_table=class_table, time_table=time_table)


HIGHEST = lax.Precision.HIGHEST

@jax.custom_vjp
def low(v):
    return lax.optimization_barrier(v.astype(jnp.bfloat16)).astype(jnp.float32)

@jax.custom_vjp
def low_back(v):
    return v

def low_keep(v):
    return (low(v), None)

def low_pass(kept, grad):
    return (grad,)

def back_keep(v):
    return (v, None)

def back_low(kept, grad):
    return (low(grad),)
low.defvjp(low_keep, low_pass)
low_back.defvjp(back_keep, back_low)

def layer_norm(values):
    centered = values - lax.optimization_barrier(jnp.mean(values, axis=-1, keepdims=True))
    variance = lax.optimization_barrier(jnp.mean(centered * centered, axis=-1, keepdims=True))
    return centered * lax.rsqrt(variance + 1e-06)

def block_forward(hidden, condition, params):
    mod_weight, mod_bias, heads_weight, heads_bias, mixing_weight, mixing_bias, up_weight, up_bias, down_weight, down_bias = params
    group_size = condition.shape[0]
    model_width = hidden.shape[-1]
    silu_cond = low(jax.nn.silu(condition))
    modulation = low_back(jnp.dot(silu_cond, mod_weight, precision=HIGHEST) + mod_bias)
    pieces = [modulation[:, number * model_width:(number + 1) * model_width][:, None, :] for number in range(6)]
    shift_one, scale_one, gate_one, shift_two, scale_two, gate_two = pieces
    states = hidden.reshape(group_size, SEQ, model_width)
    heads_in = low(layer_norm(states) * (1.0 + scale_one) + shift_one)
    projected = jnp.einsum('bsd,dce->bsce', heads_in, heads_weight, precision=HIGHEST)
    shape_heads = (group_size, SEQ, HEADS, HEAD_DIM)
    queries = low_back(low(projected[:, :, 0] + heads_bias[0])).reshape(shape_heads)
    key_rows = low_back(low(projected[:, :, 1])).reshape(shape_heads)
    value_rows = low_back(low(projected[:, :, 2] + heads_bias[1])).reshape(shape_heads)
    scores = low_back(jnp.einsum('bqhe,bkhe->bhqk', queries, key_rows, precision=HIGHEST) * HEAD_DIM ** (-0.5))
    weights = jax.nn.softmax(scores, axis=-1)
    mixed = jnp.einsum('bhqk,bkhe->bqhe', low(weights), value_rows, precision=HIGHEST)
    attended = low_back(low(mixed)).reshape(group_size, SEQ, model_width)
    attn_out = low_back(jnp.einsum('bse,ed->bsd', attended, mixing_weight, precision=HIGHEST) + mixing_bias)
    middle = states + gate_one * attn_out
    mlp_in = low(layer_norm(middle) * (1.0 + scale_two) + shift_two)
    pre_act = low_back(jnp.einsum('bsd,df->bsf', mlp_in, up_weight, precision=HIGHEST) + up_bias)
    activated = low(jax.nn.gelu(pre_act, approximate=True))
    mlp_out = low_back(jnp.einsum('bsf,fd->bsd', activated, down_weight, precision=HIGHEST) + down_bias)
    result = middle + gate_two * mlp_out
    return result.reshape(group_size * SEQ, model_width)

def reference(hidden_in, out_cotangent, class_label, time_step, modulation_weight, modulation_bias, heads_weight, heads_bias, mixing_weight, mixing_bias, up_weight, up_bias, down_weight, down_bias, class_table, time_table):
    params = tuple((member.astype(jnp.float32) for member in (modulation_weight, modulation_bias, heads_weight, heads_bias, mixing_weight, mixing_bias, up_weight, up_bias, down_weight, down_bias)))
    tables = (class_table.astype(jnp.float32), time_table.astype(jnp.float32))
    group_size = math.gcd(LATENTS, 16)
    blocks = LATENTS // group_size
    model_width = hidden_in.shape[1]
    states = hidden_in.astype(jnp.float32).reshape(blocks, group_size * SEQ, model_width)
    upstream = out_cotangent.astype(jnp.float32).reshape(blocks, group_size * SEQ, model_width)
    labels = class_label.astype(jnp.int32).reshape(blocks, group_size)
    steps_all = time_step.astype(jnp.int32).reshape(blocks, group_size)

    def one_block(running, scanned):
        block_states, block_up, block_labels, block_steps = scanned

        def run(values, table_pair, weights_all):
            condition = jnp.take(table_pair[0], block_labels, axis=0) + jnp.take(table_pair[1], block_steps, axis=0)
            return block_forward(values, condition, weights_all)
        result, pullback = jax.vjp(run, block_states, tables, params)
        grad_states, grad_tables, grad_params = pullback(block_up)
        running = jax.tree.map(lambda running_sum, addend: running_sum + addend, running, (grad_tables, grad_params))
        return (running, (result.astype(jnp.bfloat16), grad_states))
    zeros_init = jax.tree.map(jnp.zeros_like, (tables, params))
    (grad_tables, grad_params), (results, grad_states) = lax.scan(one_block, zeros_init, (states, upstream, labels, steps_all))
    return (results.reshape(-1, model_width), grad_states.reshape(-1, model_width), grad_params[0], grad_params[1], grad_params[2], grad_params[3], grad_params[4], grad_params[5], grad_params[6], grad_params[7], grad_params[8], grad_params[9], grad_tables[0], grad_tables[1])
```

```python
import jax
import jax.numpy as jnp
from jax import lax
from jax.experimental import pallas as pl
from jax.experimental.pallas import tpu as pltpu
from jax.sharding import PartitionSpec as P

SEQ = 256
HEAD_DIM = 64
F32 = jnp.float32
BF16 = jnp.bfloat16


def layer_norm(values):
    centered = values - jnp.mean(values, axis=-1, keepdims=True)
    variance = jnp.mean(centered * centered, axis=-1, keepdims=True)
    inverse = lax.rsqrt(variance + 1e-06)
    return (centered * inverse, inverse)


def norm_back(upstream, normed, inverse):
    mean_grad = jnp.mean(upstream, axis=-1, keepdims=True)
    mean_proj = jnp.mean(upstream * normed, axis=-1, keepdims=True)
    return inverse * (upstream - mean_grad - normed * mean_proj)


def gelu_tanh(values):
    return jax.nn.gelu(values, approximate=True)


def swap(values, size, bit):
    return lax.ppermute(values, "tensor", [(at, at ^ bit) for at in range(size)])


def chip_pair(own, size, axis):
    far = lax.axis_index("tensor") >= 2
    across = swap(own, size, 2)
    return jnp.concatenate(
        [jnp.where(far, across, own), jnp.where(far, own, across)], axis=axis
    )


VMEM_LIMIT = 48 * 1024 * 1024
IN_VMEM = pl.BlockSpec(memory_space=pltpu.VMEM)
IN_SMEM = pl.BlockSpec(memory_space=pltpu.SMEM)


def call(kernel, out_shape, operands, scalars=1):
    return pl.pallas_call(
        kernel,
        out_shape=out_shape,
        in_specs=[IN_SMEM] * scalars + [IN_VMEM] * (len(operands) - scalars),
        out_specs=jax.tree.map(lambda leaf: IN_VMEM, out_shape),
        compiler_params=pltpu.CompilerParams(vmem_limit_bytes=VMEM_LIMIT),
    )(*operands)


def join_rows_kernel(odd_ref, own_ref, beside_ref, out_ref):
    half = own_ref.shape[0]
    odd = odd_ref[0] == 1
    own = own_ref[...].astype(BF16)
    beside = beside_ref[...].astype(BF16)
    out_ref[0:half, :] = jnp.where(odd, beside, own)
    out_ref[half : 2 * half, :] = jnp.where(odd, own, beside)


def mixing_kernel(odd_ref, own_ref, beside_ref, weight_ref, bias_ref, out_ref):
    half = own_ref.shape[1]
    odd = odd_ref[0] == 1
    own = own_ref[...].astype(BF16)
    beside = beside_ref[...].astype(BF16)
    low = jnp.where(odd, beside, own)
    high = jnp.where(odd, own, beside)
    out_ref[...] = (
        jnp.dot(low, weight_ref[0:half, :], preferred_element_type=F32)
        + jnp.dot(high, weight_ref[half : 2 * half, :], preferred_element_type=F32)
        + bias_ref[...].astype(F32)
    )


def modulation_grad_kernel(mods_ref, silu_ref, weight_ref, weight_grad_ref, bias_grad_ref, silu_grad_ref):
    mods = mods_ref[...].astype(BF16)
    weight_grad_ref[...] = lax.dot_general(
        silu_ref[...], mods, (((0,), (0,)), ((), ())), preferred_element_type=F32
    )
    bias_grad_ref[...] = jnp.sum(mods.astype(F32), axis=0, keepdims=True)
    silu_grad_ref[...] = lax.dot_general(
        mods, weight_ref[...], (((1,), (1,)), ((), ())), preferred_element_type=F32
    )


def reduce_rows(part, size):
    odd = lax.axis_index("tensor") % 2
    half = part.shape[0] // 2
    mine = lax.dynamic_slice_in_dim(part, odd * half, half)
    theirs = lax.dynamic_slice_in_dim(part, (1 - odd) * half, half)
    chip_sum = mine + swap(theirs, size, 1)
    full = chip_sum + swap(chip_sum, size, 2)
    other = swap(full, size, 1)
    flip = odd == 1
    return jnp.concatenate([jnp.where(flip, other, full), jnp.where(flip, full, other)], axis=0)


def on_device(
    tensor_size,
    dp_size,
    hidden_in,
    out_cotangent,
    class_label,
    time_step,
    modulation_weight,
    modulation_bias,
    heads_weight,
    heads_bias,
    mixing_weight,
    mixing_bias,
    up_weight,
    up_bias,
    down_weight,
    down_bias,
    class_table,
    time_table,
):
    model_width = hidden_in.shape[1]
    own_latents = hidden_in.shape[0] // SEQ
    tok_rows = own_latents * SEQ
    heads_here = heads_weight.shape[2] // HEAD_DIM
    score_scale = HEAD_DIM ** (-0.5)
    lat_first = lax.axis_index("dp") * own_latents

    cond_part = jnp.take(class_table, class_label, axis=0).astype(F32) + jnp.take(
        time_table, time_step, axis=0
    ).astype(F32)
    condition = lax.all_gather(cond_part, "tensor", axis=1, tiled=True)
    silu_all = jax.nn.silu(condition).astype(BF16)
    silu_own = lax.dynamic_slice_in_dim(silu_all, lat_first, own_latents)
    mod_part = jnp.dot(silu_own, modulation_weight, preferred_element_type=F32) + modulation_bias.astype(F32)
    modulation = lax.all_gather(mod_part, "tensor", axis=1, tiled=True)
    pieces = [
        modulation[:, number * model_width : (number + 1) * model_width][:, None, :]
        for number in range(6)
    ]
    shift_one, scale_one, gate_one, shift_two, scale_two, gate_two = pieces

    odd_flag = (lax.axis_index("tensor") % 2).reshape(1)
    mixing_pair = chip_pair(mixing_weight.astype(F32), tensor_size, 0)
    mixing_full = call(
        join_rows_kernel,
        jax.ShapeDtypeStruct((model_width, model_width), BF16),
        (odd_flag, mixing_pair, swap(mixing_pair, tensor_size, 1)),
    )

    states = hidden_in.astype(F32).reshape(own_latents, SEQ, model_width)
    normed_one, inverse_one = layer_norm(states)
    heads_in = (normed_one * (1.0 + scale_one) + shift_one).astype(BF16)
    projected = jnp.einsum("bsd,dce->bsce", heads_in, heads_weight, preferred_element_type=F32)
    head_terms = heads_bias.astype(F32)
    shape_heads = (own_latents, SEQ, heads_here, HEAD_DIM)
    queries = (projected[:, :, 0] + head_terms[0]).astype(BF16).reshape(shape_heads)
    key_rows = projected[:, :, 1].astype(BF16).reshape(shape_heads)
    value_rows = (projected[:, :, 2] + head_terms[1]).astype(BF16).reshape(shape_heads)
    scores = jnp.einsum("bqhe,bkhe->bhqk", queries, key_rows, preferred_element_type=F32) * score_scale
    row_max = jnp.max(scores, axis=-1, keepdims=True)
    exp_terms = jnp.exp(scores - row_max)
    row_total = jnp.sum(exp_terms, axis=-1, keepdims=True)
    weights_full = exp_terms / row_total
    weights_low = weights_full.astype(BF16)
    attended = (
        jnp.einsum("bhqk,bkhe->bqhe", weights_low, value_rows, preferred_element_type=F32)
        .astype(BF16)
        .reshape(tok_rows, heads_here * HEAD_DIM)
    )
    attended_pair = chip_pair(attended.astype(F32), tensor_size, 1)
    attn_out = call(
        mixing_kernel,
        jax.ShapeDtypeStruct((tok_rows, model_width), F32),
        (
            odd_flag,
            attended_pair,
            swap(attended_pair, tensor_size, 1),
            mixing_full,
            mixing_bias.reshape(1, model_width),
        ),
    ).reshape(own_latents, SEQ, model_width)
    middle = states + gate_one * attn_out
    normed_two, inverse_two = layer_norm(middle)
    mlp_in = (normed_two * (1.0 + scale_two) + shift_two).astype(BF16).reshape(tok_rows, model_width)
    pre_act = jnp.dot(mlp_in, up_weight, preferred_element_type=F32) + up_bias.astype(F32)
    upstream = out_cotangent.astype(F32).reshape(own_latents, SEQ, model_width)
    d_mlp = (upstream * gate_two).astype(BF16).reshape(tok_rows, model_width)
    d_act = jnp.einsum("td,fd->tf", d_mlp, down_weight, preferred_element_type=F32)
    activated, gelu_pull = jax.vjp(gelu_tanh, pre_act)
    activated = activated.astype(BF16)
    d_pre = gelu_pull(d_act)[0].astype(BF16)
    d_mlp_part = jnp.einsum("tf,df->td", d_pre, up_weight, preferred_element_type=F32)
    d_mlp_in = reduce_rows(d_mlp_part, tensor_size).reshape(own_latents, SEQ, model_width)

    mlp_part = jnp.dot(activated, down_weight, preferred_element_type=F32)
    mlp_out = (reduce_rows(mlp_part, tensor_size) + down_bias.astype(F32)).reshape(
        own_latents, SEQ, model_width
    )
    d_down_weight = jnp.einsum("tf,td->fd", activated, d_mlp, preferred_element_type=F32)
    d_up_weight = jnp.einsum("td,tf->df", mlp_in, d_pre, preferred_element_type=F32)
    d_down_bias = jnp.sum(d_mlp.astype(F32), axis=0)
    d_up_bias = jnp.sum(d_pre.astype(F32), axis=0)
    up_weight_sum, down_weight_sum = lax.psum((d_up_weight, d_down_weight), "dp")

    d_shift_two = jnp.sum(d_mlp_in, axis=1)
    d_scale_two = jnp.sum(d_mlp_in * normed_two, axis=1)
    d_middle = upstream + norm_back(d_mlp_in * (1.0 + scale_two), normed_two, inverse_two)
    d_gate_one = jnp.sum(d_middle * attn_out, axis=1)
    d_attn = (d_middle * gate_one).astype(BF16).reshape(tok_rows, model_width)
    d_mixing_weight = jnp.einsum("te,td->ed", attended, d_attn, preferred_element_type=F32)
    d_mixing_bias = jnp.sum(d_attn.astype(F32), axis=0)
    d_attended = (
        jnp.einsum("td,ed->te", d_attn, mixing_weight, preferred_element_type=F32)
        .astype(BF16)
        .reshape(shape_heads)
    )
    d_weights = jnp.einsum("bqhe,bkhe->bhqk", d_attended, value_rows, preferred_element_type=F32)
    row_dots = jnp.sum(weights_full * d_weights, axis=-1, keepdims=True)
    d_scores = (weights_full * (d_weights - row_dots)).astype(BF16)
    flat_heads = (own_latents, SEQ, heads_here * HEAD_DIM)
    d_queries = (
        (jnp.einsum("bhqk,bkhe->bqhe", d_scores, key_rows, preferred_element_type=F32) * score_scale)
        .astype(BF16)
        .reshape(flat_heads)
    )
    d_keys = (
        (jnp.einsum("bhqk,bqhe->bkhe", d_scores, queries, preferred_element_type=F32) * score_scale)
        .astype(BF16)
        .reshape(flat_heads)
    )
    d_values = (
        jnp.einsum("bhqk,bqhe->bkhe", weights_low, d_attended, preferred_element_type=F32)
        .astype(BF16)
        .reshape(flat_heads)
    )
    d_stack = jnp.stack([d_queries, d_keys, d_values], axis=2)
    d_heads_weight = jnp.einsum("bsd,bsce->dce", heads_in, d_stack, preferred_element_type=F32)
    d_heads_bias = jnp.stack(
        [jnp.sum(d_queries.astype(F32), axis=(0, 1)), jnp.sum(d_values.astype(F32), axis=(0, 1))]
    )
    d_heads_part = jnp.einsum("bsce,dce->bsd", d_stack, heads_weight, preferred_element_type=F32)
    d_heads_in = reduce_rows(d_heads_part.reshape(tok_rows, model_width), tensor_size).reshape(
        own_latents, SEQ, model_width
    )
    heads_weight_sum, mixing_weight_sum = lax.psum((d_heads_weight, d_mixing_weight), "dp")
    heads_bias_sum, mixing_bias_sum, up_bias_sum, down_bias_sum = lax.psum(
        (d_heads_bias, d_mixing_bias, d_up_bias, d_down_bias), "dp"
    )
    block_out = (middle + gate_two * mlp_out).reshape(tok_rows, model_width).astype(BF16)
    d_gate_two = jnp.sum(upstream * mlp_out, axis=1)

    d_shift_one = jnp.sum(d_heads_in, axis=1)
    d_scale_one = jnp.sum(d_heads_in * normed_one, axis=1)
    input_grad = (
        d_middle + norm_back(d_heads_in * (1.0 + scale_one), normed_one, inverse_one)
    ).reshape(tok_rows, model_width)
    d_modulation = jnp.concatenate(
        [d_shift_one, d_scale_one, d_gate_one, d_shift_two, d_scale_two, d_gate_two], axis=1
    )
    own_cols = modulation_weight.shape[1]
    own_mods = lax.dynamic_slice_in_dim(d_modulation, lax.axis_index("tensor") * own_cols, own_cols, 1)
    all_mods = lax.all_gather(own_mods, "dp", axis=0, tiled=True)
    mod_weight_sum, mod_bias_row, d_silu_part = call(
        modulation_grad_kernel,
        (
            jax.ShapeDtypeStruct((model_width, own_cols), F32),
            jax.ShapeDtypeStruct((1, own_cols), F32),
            jax.ShapeDtypeStruct((all_mods.shape[0], model_width), F32),
        ),
        (all_mods, silu_all, modulation_weight),
        scalars=0,
    )
    mod_bias_sum = mod_bias_row.reshape(own_cols)
    d_silu_own = lax.psum_scatter(d_silu_part, "tensor", scatter_dimension=1, tiled=True)
    sigmoid_part = jax.nn.sigmoid(cond_part)
    d_condition = d_silu_own * sigmoid_part * (1.0 + cond_part * (1.0 - sigmoid_part))
    class_sum = jax.ops.segment_sum(d_condition, class_label, num_segments=class_table.shape[0])
    time_sum = jax.ops.segment_sum(d_condition, time_step, num_segments=time_table.shape[0])
    return (
        block_out,
        input_grad,
        mod_weight_sum,
        mod_bias_sum,
        heads_weight_sum,
        heads_bias_sum,
        mixing_weight_sum,
        mixing_bias_sum,
        up_weight_sum,
        up_bias_sum,
        down_weight_sum,
        down_bias_sum,
        class_sum,
        time_sum,
    )


def solution(mesh):
    in_specs = (
        P("dp", None),
        P("dp", None),
        P(),
        P(),
        P(None, "tensor"),
        P("tensor"),
        P(None, None, "tensor"),
        P(None, "tensor"),
        P("tensor", None),
        P(),
        P(None, "tensor"),
        P("tensor"),
        P("tensor", None),
        P(),
        P(None, "tensor"),
        P(None, "tensor"),
    )
    out_specs = (
        P("dp", None),
        P("dp", None),
        P(None, "tensor"),
        P("tensor"),
        P(None, None, "tensor"),
        P(None, "tensor"),
        P("tensor", None),
        P(),
        P(None, "tensor"),
        P("tensor"),
        P("tensor", None),
        P(),
        P(None, "tensor"),
        P(None, "tensor"),
    )

    def run(*args):
        return on_device(mesh.shape["tensor"], mesh.shape["dp"], *args)

    return jax.shard_map(run, mesh=mesh, in_specs=in_specs, out_specs=out_specs, check_vma=False)
```

```python
import functools

import jax
import jax.numpy as jnp
from jax import lax
from jax.experimental import pallas as pl
from jax.experimental.pallas import tpu as pltpu
from jax.sharding import PartitionSpec as P

SEQ = 256
HEAD_DIM = 64
F32 = jnp.float32
BF16 = jnp.bfloat16


def layer_norm(values):
    centered = values - jnp.mean(values, axis=-1, keepdims=True)
    variance = jnp.mean(centered * centered, axis=-1, keepdims=True)
    inverse = lax.rsqrt(variance + 1e-06)
    return (centered * inverse, inverse)


def norm_back(upstream, normed, inverse):
    mean_grad = jnp.mean(upstream, axis=-1, keepdims=True)
    mean_proj = jnp.mean(upstream * normed, axis=-1, keepdims=True)
    return inverse * (upstream - mean_grad - normed * mean_proj)


def gelu_tanh(values):
    return jax.nn.gelu(values, approximate=True)


def swap(values, size, bit):
    return lax.ppermute(values, "tensor", [(at, at ^ bit) for at in range(size)])


def chip_pair(own, size, axis):
    far = lax.axis_index("tensor") >= 2
    across = swap(own, size, 2)
    return jnp.concatenate(
        [jnp.where(far, across, own), jnp.where(far, own, across)], axis=axis
    )


def ring_place(size):
    order = list(range(0, size, 2)) + list(range(size - 1, 0, -2))
    index = lax.axis_index("dp")
    place = jnp.where(index % 2 == 0, index // 2, size - 1 - index // 2)
    return order, place


def gather_latents(own, size):
    if size % 2 or size > 16:
        return lax.all_gather(own, "dp", axis=0, tiled=True)
    rows = own.shape[0]
    index = lax.axis_index("dp")
    other = lax.ppermute(own, "dp", [(at, at ^ 1) for at in range(size)])
    odd = index % 2 == 1
    pair = jnp.concatenate([jnp.where(odd, other, own), jnp.where(odd, own, other)], axis=0)
    out = jnp.zeros((size * rows, own.shape[1]), own.dtype)
    out = lax.dynamic_update_slice_in_dim(out, pair, (index // 2) * 2 * rows, 0)
    for step in range(2, size, 2):
        got = lax.ppermute(pair, "dp", [(at, (at + step) % size) for at in range(size)])
        out = lax.dynamic_update_slice_in_dim(out, got, (((index - step) % size) // 2) * 2 * rows, 0)
    return out


def scatter_features(part, size):
    index = lax.axis_index("tensor")
    columns = part.shape[1] // size
    block = lambda at: lax.dynamic_slice_in_dim(part, at * columns, columns, 1)
    total = block(index)
    for bit in range(1, size):
        total = total + swap(block(index ^ bit), size, bit)
    return total


VMEM_LIMIT = 20 * 1024 * 1024
IN_VMEM = pl.BlockSpec(memory_space=pltpu.VMEM)
IN_SMEM = pl.BlockSpec(memory_space=pltpu.SMEM)


def call(kernel, out_shape, operands, scalars=1):
    return pl.pallas_call(
        kernel,
        out_shape=out_shape,
        in_specs=[IN_SMEM] * scalars + [IN_VMEM] * (len(operands) - scalars),
        out_specs=[IN_VMEM] * len(out_shape) if isinstance(out_shape, tuple) else IN_VMEM,
        compiler_params=pltpu.CompilerParams(vmem_limit_bytes=VMEM_LIMIT),
    )(*operands)


def natural(blocks):
    index = lax.axis_index("tensor")
    low, high = index % 2 == 1, index >= 2
    return [
        jnp.where(
            high,
            jnp.where(low, blocks[at ^ 3], blocks[at ^ 2]),
            jnp.where(low, blocks[at ^ 1], blocks[at]),
        )
        for at in range(4)
    ]


def join_columns(own, size):
    blocks = [own] + [swap(own, size, bit) for bit in range(1, size)]
    return jnp.concatenate(natural(blocks), axis=1)


def place_kernel(count, spots_ref, *refs):
    pieces, out_ref, sems = refs[:count], refs[count], refs[count + 1]
    rows = pieces[0].shape[0]
    copies = []
    for at in range(count):
        start = pl.multiple_of(spots_ref[at] * rows, 8)
        copies.append(
            pltpu.make_async_copy(pieces[at], out_ref.at[pl.ds(start, rows), :], sems.at[at])
        )
    for copy in copies:
        copy.start()
    for copy in copies:
        copy.wait()


def place_rows(pieces, spots):
    count = len(pieces)
    rows, columns = pieces[0].shape
    return pl.pallas_call(
        functools.partial(place_kernel, count),
        out_shape=jax.ShapeDtypeStruct((count * rows, columns), F32),
        in_specs=[IN_SMEM] + [IN_VMEM] * count,
        out_specs=pl.BlockSpec(memory_space=pl.ANY),
        scratch_shapes=[pltpu.SemaphoreType.DMA((count,))],
        compiler_params=pltpu.CompilerParams(vmem_limit_bytes=VMEM_LIMIT),
    )(jnp.stack(spots).astype(jnp.int32), *(in_vmem(piece) for piece in pieces))


def in_vmem(values):
    return pltpu.with_memory_space_constraint(values, pltpu.VMEM)


def add_kernel(spots_ref, *refs):
    count = len(refs) // 3
    for at in range(count):
        moved_ref, part_ref, out_ref = refs[at], refs[count + at], refs[2 * count + at]
        rows = moved_ref.shape[0]
        start = pl.multiple_of(spots_ref[at] * rows, 8)
        out_ref[...] = moved_ref[...] + part_ref[pl.ds(start, rows), :]


def add_pieces(moving, parts, spots):
    return call(
        add_kernel,
        tuple(pltpu.VMEM(held.shape, F32) for held in moving),
        (jnp.stack(spots).astype(jnp.int32), *(in_vmem(held) for held in moving), *(in_vmem(part) for part in parts)),
    )


def ring_spots(ways, size):
    order, place = ring_place(size)
    return lambda steps: [(place - way * steps) % size for way in ways]


class Ring:
    def __init__(self, parts, firsts, ways, size):
        order, place = ring_place(size)
        self.perms = [[(order[at], order[(at + way) % size]) for at in range(size)] for way in ways]
        self.spots = ring_spots(ways, size)
        self.parts, self.size, self.count = parts, size, 0
        self.moving = list(firsts)
        self.pieces = []

    def step(self, gate=None):
        if self.count == 2 * self.size - 2:
            return self.moving[0]
        self.count += 1
        self.moving = [lax.ppermute(held, "dp", perm) for held, perm in zip(self.moving, self.perms)]
        if gate is not None:
            self.moving = after(self.moving, gate)
        if self.count < self.size:
            self.moving = add_pieces(self.moving, self.parts, self.spots(self.count))
        if self.count >= self.size - 1:
            self.pieces.append(self.moving)
        return self.moving[0]

    def finish(self):
        while self.count < 2 * self.size - 2:
            self.step()
        last = [self.spots(self.size - 1 + step) for step in range(self.size)]
        return [
            place_rows(kept, [spots[at] for spots in last])
            for at, kept in enumerate(zip(*self.pieces))
        ]


class Plain:
    def __init__(self, parts):
        self.parts = parts

    def step(self, gate=None):
        return self.parts[0]

    def finish(self):
        return lax.psum(self.parts, "dp")


def start_sum(parts, firsts, ways, size):
    whole = all(part.shape[0] % (8 * size) == 0 for part in parts)
    return Ring(parts, firsts, ways, size) if whole and size <= 16 else Plain(parts)


def join_rows_kernel(odd_ref, own_ref, beside_ref, out_ref):
    half = own_ref.shape[0]
    odd = odd_ref[0] == 1
    own = own_ref[...].astype(BF16)
    beside = beside_ref[...].astype(BF16)
    out_ref[0:half, :] = jnp.where(odd, beside, own)
    out_ref[half : 2 * half, :] = jnp.where(odd, own, beside)


def mixing_kernel(odd_ref, own_ref, beside_ref, weight_ref, bias_ref, out_ref):
    half = own_ref.shape[1]
    odd = odd_ref[0] == 1
    own = own_ref[...].astype(BF16)
    beside = beside_ref[...].astype(BF16)
    low = jnp.where(odd, beside, own)
    high = jnp.where(odd, own, beside)
    out_ref[...] = (
        jnp.dot(low, weight_ref[0:half, :], preferred_element_type=F32)
        + jnp.dot(high, weight_ref[half : 2 * half, :], preferred_element_type=F32)
        + bias_ref[...].astype(F32)
    )


def column_sums(values):
    return jnp.sum(values.astype(F32), axis=0, keepdims=True)


def over_tokens(left, right):
    return lax.dot_general(left, right, (((0,), (0,)), ((), ())), preferred_element_type=F32)


def copy_block(spots_ref, at, part_ref, first_ref):
    rows = first_ref.shape[0]
    first_ref[...] = part_ref[pl.ds(pl.multiple_of(spots_ref[at] * rows, 8), rows), :]


def mlp_grads_kernel(
    spots_ref, mlp_in_ref, d_pre_ref, activated_ref, d_mlp_ref, up_ref, down_ref, bias_ref, up_first_ref, down_first_ref
):
    up_ref[...] = over_tokens(mlp_in_ref[...], d_pre_ref[...])
    down_ref[...] = over_tokens(activated_ref[...], d_mlp_ref[...])
    bias_ref[0:1, :] = column_sums(d_pre_ref[...])
    bias_ref[1:2, :] = column_sums(d_mlp_ref[...])
    copy_block(spots_ref, 0, up_ref, up_first_ref)
    copy_block(spots_ref, 1, down_ref, down_first_ref)


def attention_grads_kernel(
    spots_ref,
    heads_in_ref,
    d_queries_ref,
    d_keys_ref,
    d_values_ref,
    attended_ref,
    d_attn_ref,
    bias_ref,
    upper_ref,
    lower_ref,
    upper_first_ref,
    lower_first_ref,
):
    feats = d_queries_ref.shape[1]
    width = heads_in_ref.shape[1]
    heads_in = heads_in_ref[...]
    upper_ref[0:feats, :] = over_tokens(d_queries_ref[...], heads_in)
    upper_ref[feats : 2 * feats, :] = over_tokens(d_keys_ref[...], heads_in)
    lower_ref[0:feats, :] = over_tokens(d_values_ref[...], heads_in)
    lower_ref[feats : 2 * feats, :] = over_tokens(attended_ref[...], d_attn_ref[...])
    base = 2 * feats
    lower_ref[base:, :] = jnp.zeros((lower_ref.shape[0] - base, width), F32)
    lower_ref[base : base + 2, :] = bias_ref[...]
    lower_ref[base + 2 : base + 3, :] = column_sums(d_attn_ref[...])
    lower_ref[base + 3 : base + 4, 0:feats] = column_sums(d_queries_ref[...])
    lower_ref[base + 4 : base + 5, 0:feats] = column_sums(d_values_ref[...])
    copy_block(spots_ref, 0, upper_ref, upper_first_ref)
    copy_block(spots_ref, 1, lower_ref, lower_first_ref)


def modulation_grad_kernel(mods_ref, silu_ref, weight_ref, weight_grad_ref, bias_grad_ref, silu_grad_ref):
    mods = mods_ref[...].astype(BF16)
    weight_grad_ref[...] = lax.dot_general(
        silu_ref[...], mods, (((0,), (0,)), ((), ())), preferred_element_type=F32
    )
    bias_grad_ref[...] = jnp.sum(mods.astype(F32), axis=0, keepdims=True)
    silu_grad_ref[...] = lax.dot_general(
        mods, weight_ref[...], (((1,), (1,)), ((), ())), preferred_element_type=F32
    )


def after(values, gate):
    flat, tree = jax.tree.flatten(values)
    return jax.tree.unflatten(tree, lax.optimization_barrier((*flat, gate))[:-1])


def chip_rows(part, size):
    odd = lax.axis_index("tensor") % 2
    half = part.shape[0] // 2
    mine = lax.dynamic_slice_in_dim(part, odd * half, half)
    theirs = lax.dynamic_slice_in_dim(part, (1 - odd) * half, half)
    return mine + swap(theirs, size, 1)


def whole_rows(full, size):
    other = swap(full, size, 1)
    flip = lax.axis_index("tensor") % 2 == 1
    return jnp.concatenate([jnp.where(flip, other, full), jnp.where(flip, full, other)], axis=0)


def on_device(
    tensor_size,
    dp_size,
    hidden_in,
    out_cotangent,
    class_label,
    time_step,
    modulation_weight,
    modulation_bias,
    heads_weight,
    heads_bias,
    mixing_weight,
    mixing_bias,
    up_weight,
    up_bias,
    down_weight,
    down_bias,
    class_table,
    time_table,
):
    model_width = hidden_in.shape[1]
    own_latents = hidden_in.shape[0] // SEQ
    tok_rows = own_latents * SEQ
    heads_here = heads_weight.shape[2] // HEAD_DIM
    score_scale = HEAD_DIM ** (-0.5)
    lat_first = lax.axis_index("dp") * own_latents

    class_pick = jax.nn.one_hot(class_label, class_table.shape[0], dtype=BF16)
    time_pick = jax.nn.one_hot(time_step, time_table.shape[0], dtype=BF16)
    cond_part = jnp.dot(class_pick, class_table, preferred_element_type=F32) + jnp.dot(
        time_pick, time_table, preferred_element_type=F32
    )
    condition = join_columns(cond_part, tensor_size)
    silu_all = jax.nn.silu(condition).astype(BF16)
    silu_own = lax.dynamic_slice_in_dim(silu_all, lat_first, own_latents)
    mod_part = jnp.dot(silu_own, modulation_weight, preferred_element_type=F32) + modulation_bias.astype(F32)
    modulation = join_columns(mod_part, tensor_size)
    pieces = [
        modulation[:, number * model_width : (number + 1) * model_width][:, None, :]
        for number in range(6)
    ]
    shift_one, scale_one, gate_one, shift_two, scale_two, gate_two = pieces

    odd_flag = (lax.axis_index("tensor") % 2).reshape(1)
    mixing_pair = chip_pair(after(mixing_weight, cond_part).astype(F32), tensor_size, 0)
    mixing_full = call(
        join_rows_kernel,
        jax.ShapeDtypeStruct((model_width, model_width), BF16),
        (odd_flag, mixing_pair, swap(mixing_pair, tensor_size, 1)),
    )

    states = hidden_in.astype(F32).reshape(own_latents, SEQ, model_width)
    normed_one, inverse_one = layer_norm(states)
    heads_in = (normed_one * (1.0 + scale_one) + shift_one).astype(BF16)
    projected = jnp.einsum("bsd,dce->bsce", heads_in, heads_weight, preferred_element_type=F32)
    head_terms = heads_bias.astype(F32)
    shape_heads = (own_latents, SEQ, heads_here, HEAD_DIM)
    queries = (projected[:, :, 0] + head_terms[0]).astype(BF16).reshape(shape_heads)
    key_rows = projected[:, :, 1].astype(BF16).reshape(shape_heads)
    value_rows = (projected[:, :, 2] + head_terms[1]).astype(BF16).reshape(shape_heads)
    scores = jnp.einsum("bqhe,bkhe->bhqk", queries, key_rows, preferred_element_type=F32) * score_scale
    row_max = jnp.max(scores, axis=-1, keepdims=True)
    exp_terms = jnp.exp(scores - row_max)
    row_total = jnp.sum(exp_terms, axis=-1, keepdims=True)
    weights_full = exp_terms / row_total
    weights_low = weights_full.astype(BF16)
    attended = (
        jnp.einsum("bhqk,bkhe->bqhe", weights_low, value_rows, preferred_element_type=F32)
        .astype(BF16)
        .reshape(tok_rows, heads_here * HEAD_DIM)
    )
    upstream = out_cotangent.astype(F32).reshape(own_latents, SEQ, model_width)
    d_mlp = (upstream * gate_two).astype(BF16).reshape(tok_rows, model_width)
    d_act = jnp.einsum("td,fd->tf", d_mlp, down_weight, preferred_element_type=F32)
    attended_pair = chip_pair(attended.astype(F32), tensor_size, 1)
    attended_pair, mixing_full, d_act = lax.optimization_barrier((attended_pair, mixing_full, d_act))
    attn_out = call(
        mixing_kernel,
        jax.ShapeDtypeStruct((tok_rows, model_width), F32),
        (
            odd_flag,
            attended_pair,
            swap(attended_pair, tensor_size, 1),
            mixing_full,
            mixing_bias.reshape(1, model_width),
        ),
    ).reshape(own_latents, SEQ, model_width)
    middle = states + gate_one * attn_out
    normed_two, inverse_two = layer_norm(middle)
    mlp_in = (normed_two * (1.0 + scale_two) + shift_two).astype(BF16).reshape(tok_rows, model_width)
    pre_act = jnp.dot(mlp_in, up_weight, preferred_element_type=F32) + up_bias.astype(F32)
    activated, gelu_pull = jax.vjp(gelu_tanh, pre_act)
    activated = activated.astype(BF16)
    d_pre = gelu_pull(d_act)[0].astype(BF16)
    d_mlp_part = jnp.einsum("tf,df->td", d_pre, up_weight, preferred_element_type=F32)
    chip_two = chip_rows(d_mlp_part, tensor_size)

    mlp_part = jnp.dot(activated, down_weight, preferred_element_type=F32)
    activated, d_pre = after((activated, d_pre), chip_two)
    ways = (1, -1)
    first_spots = jnp.stack(ring_spots(ways, dp_size)(0)).astype(jnp.int32)
    up_part, down_part, mlp_bias, up_first, down_first = call(
        mlp_grads_kernel,
        (
            pltpu.VMEM((model_width, d_pre.shape[1]), F32),
            pltpu.VMEM((activated.shape[1], model_width), F32),
            pltpu.VMEM((2, model_width), F32),
            pltpu.VMEM((model_width // dp_size, d_pre.shape[1]), F32),
            pltpu.VMEM((activated.shape[1] // dp_size, model_width), F32),
        ),
        (first_spots, mlp_in, d_pre, activated, d_mlp),
    )
    mlp_ring = start_sum((up_part, down_part), (up_first, down_first), ways, dp_size)
    across_two = after(swap(chip_two, tensor_size, 2), mlp_ring.step())
    full_two = chip_two + across_two
    d_mlp_in = whole_rows(full_two, tensor_size).reshape(own_latents, SEQ, model_width)
    d_mlp_in = after(d_mlp_in, mlp_ring.step(full_two))
    chip_out = after(chip_rows(mlp_part, tensor_size), full_two)
    full_out = chip_out + swap(chip_out, tensor_size, 2)
    mlp_out = (whole_rows(full_out, tensor_size) + down_bias.astype(F32)).reshape(
        own_latents, SEQ, model_width
    )
    d_shift_two = jnp.sum(d_mlp_in, axis=1)
    d_scale_two = jnp.sum(d_mlp_in * normed_two, axis=1)
    d_middle = upstream + norm_back(d_mlp_in * (1.0 + scale_two), normed_two, inverse_two)
    d_gate_one = jnp.sum(d_middle * attn_out, axis=1)
    d_attn = (d_middle * gate_one).astype(BF16).reshape(tok_rows, model_width)
    d_attended = (
        jnp.einsum("td,ed->te", d_attn, mixing_weight, preferred_element_type=F32)
        .astype(BF16)
        .reshape(shape_heads)
    )
    d_attended = after(d_attended, mlp_ring.step(d_attended))
    d_weights = jnp.einsum("bqhe,bkhe->bhqk", d_attended, value_rows, preferred_element_type=F32)
    row_dots = jnp.sum(weights_full * d_weights, axis=-1, keepdims=True)
    d_scores = (weights_full * (d_weights - row_dots)).astype(BF16)
    d_scores = after(d_scores, mlp_ring.step(d_scores))
    flat_heads = (own_latents, SEQ, heads_here * HEAD_DIM)
    d_queries = (
        (jnp.einsum("bhqk,bkhe->bqhe", d_scores, key_rows, preferred_element_type=F32) * score_scale)
        .astype(BF16)
        .reshape(flat_heads)
    )
    d_keys = (
        (jnp.einsum("bhqk,bqhe->bkhe", d_scores, queries, preferred_element_type=F32) * score_scale)
        .astype(BF16)
        .reshape(flat_heads)
    )
    d_values = (
        jnp.einsum("bhqk,bqhe->bkhe", weights_low, d_attended, preferred_element_type=F32)
        .astype(BF16)
        .reshape(flat_heads)
    )
    d_stack = jnp.stack([d_queries, d_keys, d_values], axis=2)
    d_heads_part = jnp.einsum("bsce,dce->bsd", d_stack, heads_weight, preferred_element_type=F32)
    chip_one = after(
        chip_rows(d_heads_part.reshape(tok_rows, model_width), tensor_size), full_out
    )
    own_feats = heads_here * HEAD_DIM
    d_queries, d_keys, d_values = after((d_queries, d_keys, d_values), chip_one)
    upper_rows, lower_rows = 2 * own_feats, 2 * own_feats + 8 * dp_size
    upper_part, lower_part, upper_first, lower_first = call(
        attention_grads_kernel,
        (
            pltpu.VMEM((upper_rows, model_width), F32),
            pltpu.VMEM((lower_rows, model_width), F32),
            pltpu.VMEM((upper_rows // dp_size, model_width), F32),
            pltpu.VMEM((lower_rows // dp_size, model_width), F32),
        ),
        (
            first_spots,
            heads_in.reshape(tok_rows, model_width),
            d_queries.reshape(tok_rows, own_feats),
            d_keys.reshape(tok_rows, own_feats),
            d_values.reshape(tok_rows, own_feats),
            attended,
            d_attn,
            mlp_bias,
        ),
    )
    heads_ring = start_sum((upper_part, lower_part), (upper_first, lower_first), ways, dp_size)
    gate = mlp_ring.step(upper_first)
    gate = heads_ring.step(gate)
    gate = mlp_ring.step(gate)
    across_one = after(swap(chip_one, tensor_size, 2), gate)
    full_one = chip_one + across_one
    d_heads_in = whole_rows(full_one, tensor_size).reshape(own_latents, SEQ, model_width)
    d_heads_in = after(d_heads_in, heads_ring.step(full_one))
    block_out = (middle + gate_two * mlp_out).reshape(tok_rows, model_width).astype(BF16)
    d_gate_two = jnp.sum(upstream * mlp_out, axis=1)

    d_shift_one = jnp.sum(d_heads_in, axis=1)
    d_scale_one = jnp.sum(d_heads_in * normed_one, axis=1)
    input_grad = (
        d_middle + norm_back(d_heads_in * (1.0 + scale_one), normed_one, inverse_one)
    ).reshape(tok_rows, model_width)
    d_modulation = jnp.concatenate(
        [d_shift_one, d_scale_one, d_gate_one, d_shift_two, d_scale_two, d_gate_two], axis=1
    )
    own_cols = modulation_weight.shape[1]
    own_mods = lax.dynamic_slice_in_dim(d_modulation, lax.axis_index("tensor") * own_cols, own_cols, 1)
    mlp_ring.step(own_mods)
    heads_ring.step(own_mods)
    up_weight_sum, down_weight_sum = mlp_ring.finish()
    upper, lower = heads_ring.finish()
    heads_weight_sum = (
        jnp.concatenate([upper, lower[:own_feats]], axis=0)
        .reshape(3, own_feats, model_width)
        .transpose(2, 0, 1)
    )
    mixing_weight_sum = lower[own_feats : 2 * own_feats]
    up_bias_sum, down_bias_sum, mixing_bias_sum = (lower[2 * own_feats + row] for row in range(3))
    heads_bias_sum = lower[2 * own_feats + 3 : 2 * own_feats + 5, :own_feats]
    all_mods = gather_latents(own_mods, dp_size)
    mod_weight_sum, mod_bias_row, d_silu_part = call(
        modulation_grad_kernel,
        (
            jax.ShapeDtypeStruct((model_width, own_cols), F32),
            jax.ShapeDtypeStruct((1, own_cols), F32),
            jax.ShapeDtypeStruct((all_mods.shape[0], model_width), F32),
        ),
        (all_mods, silu_all, modulation_weight),
        scalars=0,
    )
    mod_bias_sum = mod_bias_row.reshape(own_cols)
    d_silu_own = scatter_features(d_silu_part, tensor_size)
    sigmoid_part = jax.nn.sigmoid(cond_part)
    d_condition = d_silu_own * sigmoid_part * (1.0 + cond_part * (1.0 - sigmoid_part))
    exact = dict(preferred_element_type=F32, precision=lax.Precision.HIGHEST)
    class_sum = jnp.einsum("lk,lf->kf", class_pick.astype(F32), d_condition, **exact)
    time_sum = jnp.einsum("lk,lf->kf", time_pick.astype(F32), d_condition, **exact)
    return (
        block_out,
        input_grad,
        mod_weight_sum,
        mod_bias_sum,
        heads_weight_sum,
        heads_bias_sum,
        mixing_weight_sum,
        mixing_bias_sum,
        up_weight_sum,
        up_bias_sum,
        down_weight_sum,
        down_bias_sum,
        class_sum,
        time_sum,
    )


def solution(mesh):
    in_specs = (
        P("dp", None),
        P("dp", None),
        P(),
        P(),
        P(None, "tensor"),
        P("tensor"),
        P(None, None, "tensor"),
        P(None, "tensor"),
        P("tensor", None),
        P(),
        P(None, "tensor"),
        P("tensor"),
        P("tensor", None),
        P(),
        P(None, "tensor"),
        P(None, "tensor"),
    )
    out_specs = (
        P("dp", None),
        P("dp", None),
        P(None, "tensor"),
        P("tensor"),
        P(None, None, "tensor"),
        P(None, "tensor"),
        P("tensor", None),
        P(),
        P(None, "tensor"),
        P("tensor"),
        P("tensor", None),
        P(),
        P(None, "tensor"),
        P(None, "tensor"),
    )

    def run(*args):
        return on_device(mesh.shape["tensor"], mesh.shape["dp"], *args)

    return jax.shard_map(run, mesh=mesh, in_specs=in_specs, out_specs=out_specs, check_vma=False)
```

```python
import functools
import math

import jax
import jax.numpy as jnp
from jax import lax
from jax.experimental import pallas as pl
from jax.experimental.pallas import tpu as pltpu
from jax.sharding import PartitionSpec as P

SEQ = 256
HEAD_DIM = 64
F32 = jnp.float32
BF16 = jnp.bfloat16


def swap(values, size, bit):
    return lax.ppermute(values, "tensor", [(at, at ^ bit) for at in range(size)])


def ring_place(size):
    order = list(range(0, size, 2)) + list(range(size - 1, 0, -2))
    index = lax.axis_index("dp")
    place = jnp.where(index % 2 == 0, index // 2, size - 1 - index // 2)
    return order, place


def gather_latents(own, size):
    if size % 2 or size > 16:
        return lax.all_gather(own, "dp", axis=0, tiled=True)
    rows = own.shape[0]
    index = lax.axis_index("dp")
    other = lax.ppermute(own, "dp", [(at, at ^ 1) for at in range(size)])
    odd = index % 2 == 1
    pair = jnp.concatenate([jnp.where(odd, other, own), jnp.where(odd, own, other)], axis=0)
    out = jnp.zeros((size * rows, own.shape[1]), own.dtype)
    out = lax.dynamic_update_slice_in_dim(out, pair, (index // 2) * 2 * rows, 0)
    for step in range(2, size, 2):
        got = lax.ppermute(pair, "dp", [(at, (at + step) % size) for at in range(size)])
        out = lax.dynamic_update_slice_in_dim(out, got, (((index - step) % size) // 2) * 2 * rows, 0)
    return out


def scatter_features(part, size):
    index = lax.axis_index("tensor")
    columns = part.shape[1] // size
    block = lambda at: lax.dynamic_slice_in_dim(part, at * columns, columns, 1)
    total = block(index)
    for bit in range(1, size):
        total = total + swap(block(index ^ bit), size, bit)
    return total


VMEM_LIMIT = 20 * 1024 * 1024
SMALL_LIMIT = 8 * 1024 * 1024
GELU_SCALE = (2.0 / math.pi) ** 0.5
IN_VMEM = pl.BlockSpec(memory_space=pltpu.VMEM)
IN_SMEM = pl.BlockSpec(memory_space=pltpu.SMEM)


QUICK = pl.CostEstimate(flops=1, transcendentals=0, bytes_accessed=1)


def call(kernel, out_shape, operands, scalars=1, scratch=(), limit=VMEM_LIMIT):
    single = not isinstance(out_shape, tuple)
    return pl.pallas_call(
        kernel,
        out_shape=out_shape,
        in_specs=[IN_SMEM] * scalars + [IN_VMEM] * (len(operands) - scalars),
        out_specs=IN_VMEM if single else [IN_VMEM] * len(out_shape),
        scratch_shapes=list(scratch),
        compiler_params=pltpu.CompilerParams(vmem_limit_bytes=limit),
        cost_estimate=QUICK,
    )(*operands)


def natural(blocks):
    index = lax.axis_index("tensor")
    low, high = index % 2 == 1, index >= 2
    return [
        jnp.where(
            high,
            jnp.where(low, blocks[at ^ 3], blocks[at ^ 2]),
            jnp.where(low, blocks[at ^ 1], blocks[at]),
        )
        for at in range(4)
    ]


def join_columns(own, size):
    blocks = [own] + [swap(own, size, bit) for bit in range(1, size)]
    return jnp.concatenate(natural(blocks), axis=1)


def place_kernel(steps, first, targets, outs, spots_ref, *refs):
    count = len(targets)
    pieces, out_refs, sems = refs[: steps * count], refs[steps * count : steps * count + outs], refs[-1]
    copies = []
    filled = [0] * outs
    for entry, runs in enumerate(targets):
        height = pieces[entry].shape[0]
        at = 0
        for share, out in runs:
            rows = height * share[0] // share[1]
            for step in range(steps):
                start = pl.multiple_of(spots_ref[first + step, entry] * rows + filled[out], 8)
                copies.append(
                    pltpu.make_async_copy(
                        pieces[step * count + entry].at[pl.ds(at, rows), :],
                        out_refs[out].at[pl.ds(start, rows), :],
                        sems.at[len(copies)],
                    )
                )
            at += rows
            filled[out] += rows * steps
    for copy in copies:
        copy.start()
    for copy in copies:
        copy.wait()


def place_rows(pieces, table, first, targets, shapes):
    steps = len(pieces)
    copies = steps * sum(len(runs) for runs in targets)
    return pl.pallas_call(
        functools.partial(place_kernel, steps, first, targets, len(shapes)),
        out_shape=[jax.ShapeDtypeStruct(shape, F32) for shape in shapes],
        in_specs=[IN_SMEM] + [IN_VMEM] * (steps * len(targets)),
        out_specs=[pl.BlockSpec(memory_space=pl.ANY)] * len(shapes),
        scratch_shapes=[pltpu.SemaphoreType.DMA((copies,))],
        compiler_params=pltpu.CompilerParams(vmem_limit_bytes=SMALL_LIMIT),
        cost_estimate=QUICK,
    )(table, *(piece for step in pieces for piece in step))


def add_kernel(step, spots_ref, *refs):
    count = len(refs) // 3
    for at in range(count):
        moved_ref, part_ref, out_ref = refs[at], refs[count + at], refs[2 * count + at]
        rows = moved_ref.shape[0]
        start = pl.multiple_of(spots_ref[step, at] * rows, 8)
        out_ref[...] = moved_ref[...] + part_ref[pl.ds(start, rows), :]


def add_pieces(moving, parts, table, step):
    return call(
        functools.partial(add_kernel, step),
        tuple(jax.ShapeDtypeStruct(held.shape, F32) for held in moving),
        (table, *moving, *parts),
        limit=SMALL_LIMIT,
    )


def ring_table(ways, size):
    order, place = ring_place(size)
    steps = jnp.arange(2 * size - 1, dtype=jnp.int32)[:, None]
    return (place - jnp.asarray(ways, jnp.int32)[None, :] * steps) % size


class Ring:
    def __init__(self, parts, firsts, ways, size, table):
        order, place = ring_place(size)
        self.perms = [[(order[at], order[(at + way) % size]) for at in range(size)] for way in ways]
        self.table = table
        self.parts, self.size, self.count = parts, size, 0
        self.moving = list(firsts)
        self.pieces = []

    def step(self, gate=None):
        if self.count == 2 * self.size - 2:
            return self.moving[0]
        self.count += 1
        self.moving = [lax.ppermute(held, "dp", perm) for held, perm in zip(self.moving, self.perms)]
        if gate is not None:
            self.moving = after(self.moving, gate)
        if self.count < self.size:
            self.moving = add_pieces(self.moving, self.parts, self.table, self.count)
        if self.count >= self.size - 1:
            self.pieces.append(self.moving)
        return self.moving[0]

    def finish(self, targets, shapes):
        while self.count < 2 * self.size - 2:
            self.step()
        return place_rows(self.pieces, self.table, self.size - 1, targets, shapes)


class Plain:
    def __init__(self, parts):
        self.parts = parts

    def step(self, gate=None):
        return self.parts[0]

    def finish(self, targets, shapes):
        outs = [[] for shape in shapes]
        for part, runs in zip(lax.psum(self.parts, "dp"), targets):
            at = 0
            for share, out in runs:
                rows = part.shape[0] * share[0] // share[1]
                outs[out].append(part[at : at + rows])
                at += rows
        return [jnp.concatenate(rows, axis=0) for rows in outs]


def whole_blocks(heights, size):
    return size <= 16 and size % 2 == 0 and all(height % (8 * size) == 0 for height in heights)


def start_sum(parts, firsts, ways, size, table, rings):
    return Ring(parts, firsts, ways, size, table) if rings else Plain(parts)


def column_sums(values):
    return jnp.sum(values.astype(F32), axis=0, keepdims=True)


def over_tokens(left, right):
    return lax.dot_general(left, right, (((0,), (0,)), ((), ())), preferred_element_type=F32)


def copy_block(spots_ref, at, part_ref, first_ref):
    rows = first_ref.shape[0]
    first_ref[...] = part_ref[pl.ds(pl.multiple_of(spots_ref[0, at] * rows, 8), rows), :]


def mlp_grads_kernel(
    spots_ref,
    flags_ref,
    mlp_in_ref,
    d_pre_ref,
    activated_ref,
    d_mlp_ref,
    down_weight_ref,
    up_ref,
    down_ref,
    bias_ref,
    up_first_ref,
    down_first_ref,
    mine_ref,
    theirs_ref,
    part_ref,
):
    up_ref[...] = over_tokens(mlp_in_ref[...], d_pre_ref[...])
    down_ref[...] = over_tokens(activated_ref[...], d_mlp_ref[...])
    bias_ref[0:1, :] = column_sums(d_pre_ref[...])
    bias_ref[1:2, :] = column_sums(d_mlp_ref[...])
    copy_block(spots_ref, 0, up_ref, up_first_ref)
    copy_block(spots_ref, 1, down_ref, down_first_ref)
    part_ref[...] = jnp.dot(activated_ref[...], down_weight_ref[...], preferred_element_type=F32)
    split_rows(flags_ref[0], part_ref, mine_ref, theirs_ref)


def attention_grads_kernel(
    blocks,
    spots_ref,
    heads_in_ref,
    d_queries_ref,
    d_keys_ref,
    d_values_ref,
    attended_ref,
    d_attn_ref,
    bias_ref,
    upper_ref,
    lower_ref,
    upper_first_ref,
    lower_first_ref,
):
    feats = d_queries_ref.shape[1]
    width = heads_in_ref.shape[1]
    heads_in = heads_in_ref[...]
    upper_ref[0:feats, :] = over_tokens(d_queries_ref[...], heads_in)
    upper_ref[feats : 2 * feats, :] = over_tokens(d_keys_ref[...], heads_in)
    values_part = over_tokens(d_values_ref[...], heads_in)
    mixing_part = over_tokens(attended_ref[...].astype(BF16), d_attn_ref[...])
    run = feats // blocks
    extra = lower_ref.shape[0] // blocks - 2 * run
    for at in range(blocks):
        base = at * (2 * run + extra)
        lower_ref[base : base + run, :] = values_part[at * run : (at + 1) * run]
        lower_ref[base + run : base + 2 * run, :] = mixing_part[at * run : (at + 1) * run]
        lower_ref[base + 2 * run : base + 2 * run + extra, :] = jnp.zeros((extra, width), F32)
    base = 2 * run
    lower_ref[base : base + 2, :] = bias_ref[...]
    lower_ref[base + 2 : base + 3, :] = column_sums(d_attn_ref[...])
    lower_ref[base + 3 : base + 4, 0:feats] = column_sums(d_queries_ref[...])
    lower_ref[base + 4 : base + 5, 0:feats] = column_sums(d_values_ref[...])
    copy_block(spots_ref, 0, upper_ref, upper_first_ref)
    copy_block(spots_ref, 1, lower_ref, lower_first_ref)


def of_rows(values):
    centered = values - jnp.mean(values, axis=-1, keepdims=True)
    inverse = lax.rsqrt(jnp.mean(centered * centered, axis=-1, keepdims=True) + 1e-06)
    return centered * inverse, inverse


def against_rows(left, right):
    return lax.dot_general(left, right, (((1,), (1,)), ((), ())), preferred_element_type=F32)


def times(left, right):
    return jnp.dot(left, right, preferred_element_type=F32)


def latent_rows(ref):
    return [slice(at * SEQ, (at + 1) * SEQ) for at in range(ref.shape[0] // SEQ)]


def head_columns(columns):
    return [slice(at * HEAD_DIM, (at + 1) * HEAD_DIM) for at in range(columns // HEAD_DIM)]


def softmax_rows(queries, key_rows):
    scores = against_rows(queries, key_rows) * HEAD_DIM ** (-0.5)
    exp_terms = jnp.exp(scores - jnp.max(scores, axis=-1, keepdims=True))
    return exp_terms / jnp.sum(exp_terms, axis=-1, keepdims=True)


def attend_kernel(
    table_ref, flags_ref, mixing_bias_ref, up_bias_ref, down_bias_ref, hidden_ref, scale_ref, shift_ref, weight_ref, bias_ref, heads_in_ref, queries_ref, keys_ref, values_ref, attended_ref
):
    feats = queries_ref.shape[1]
    bias = bias_ref[...].astype(F32)
    for at, rows in enumerate(latent_rows(hidden_ref)):
        normed, inverse = of_rows(hidden_ref[rows, :].astype(F32))
        heads_in = (normed * (1.0 + scale_ref[at : at + 1, :]) + shift_ref[at : at + 1, :]).astype(BF16)
        heads_in_ref[rows, :] = heads_in
        queries = (against_rows(heads_in, weight_ref[0:feats, :]) + bias[0:1]).astype(BF16)
        keys = against_rows(heads_in, weight_ref[feats : 2 * feats, :]).astype(BF16)
        values = (against_rows(heads_in, weight_ref[2 * feats : 3 * feats, :]) + bias[1:2]).astype(BF16)
        queries_ref[rows, :] = queries
        keys_ref[rows, :] = keys
        values_ref[rows, :] = values
        mixed = []
        for cols in head_columns(feats):
            weights = softmax_rows(queries[:, cols], keys[:, cols])
            mixed.append(times(weights.astype(BF16), values[:, cols]))
        attended_ref[rows, :] = jnp.concatenate(mixed, axis=1).astype(BF16).astype(F32)


def in_order(flags_ref, blocks):
    low, high = flags_ref[0] == 1, flags_ref[1] == 1
    return [
        jnp.where(
            high,
            jnp.where(low, blocks[at ^ 3], blocks[at ^ 2]),
            jnp.where(low, blocks[at ^ 1], blocks[at]),
        )
        for at in range(4)
    ]


def widen_kernel(values_ref, behind_ref, out_ref):
    out_ref[...] = values_ref[...].astype(F32)


def cotangent_kernel(cotangent_ref, gate_ref, down_ref, d_mlp_ref, d_act_ref):
    for at, rows in enumerate(latent_rows(cotangent_ref)):
        d_mlp = (cotangent_ref[rows, :].astype(F32) * gate_ref[at : at + 1, :]).astype(BF16)
        d_mlp_ref[rows, :] = d_mlp
        d_act_ref[rows, :] = against_rows(d_mlp, down_ref[...])


def mlp_kernel(
    odd_ref,
    own_ref,
    beside_ref,
    across_ref,
    corner_ref,
    mixing_own_ref,
    mixing_beside_ref,
    mixing_across_ref,
    mixing_corner_ref,
    mixing_bias_ref,
    hidden_ref,
    gate_ref,
    scale_ref,
    shift_ref,
    up_ref,
    up_bias_ref,
    d_act_ref,
    attn_out_ref,
    mlp_in_ref,
    activated_ref,
    d_pre_ref,
    mine_ref,
    theirs_ref,
    part_ref,
):
    odd = odd_ref[0]
    blocks = (own_ref, beside_ref, across_ref, corner_ref)
    mixing = in_order(
        odd_ref,
        [ref[...].astype(BF16) for ref in (mixing_own_ref, mixing_beside_ref, mixing_across_ref, mixing_corner_ref)],
    )
    for at, rows in enumerate(latent_rows(hidden_ref)):
        attn_out = mixing_bias_ref[...].astype(F32)
        for block, piece in enumerate(in_order(odd_ref, [ref[rows, :] for ref in blocks])):
            attn_out = attn_out + times(piece.astype(BF16), mixing[block])
        attn_out_ref[rows, :] = attn_out
        middle = hidden_ref[rows, :].astype(F32) + gate_ref[at : at + 1, :] * attn_out
        normed, inverse = of_rows(middle)
        mlp_in = (normed * (1.0 + scale_ref[at : at + 1, :]) + shift_ref[at : at + 1, :]).astype(BF16)
        mlp_in_ref[rows, :] = mlp_in
        pre_act = times(mlp_in, up_ref[...]) + up_bias_ref[...].astype(F32)
        square = pre_act * pre_act
        bend = jnp.tanh(GELU_SCALE * pre_act * (1.0 + 0.044715 * square))
        activated_ref[rows, :] = (0.5 * pre_act * (1.0 + bend)).astype(BF16)
        slope = 0.5 * (1.0 + bend) + 0.5 * pre_act * (1.0 - bend * bend) * (
            GELU_SCALE * (1.0 + 3.0 * 0.044715 * square)
        )
        d_pre = (d_act_ref[rows, :] * slope).astype(BF16)
        d_pre_ref[rows, :] = d_pre
        part_ref[rows, :] = against_rows(d_pre, up_ref[...])
    split_rows(odd, part_ref, mine_ref, theirs_ref)


def split_rows(odd, part_ref, mine_ref, theirs_ref):
    half = mine_ref.shape[0]
    mine_ref[...] = part_ref[pl.ds(pl.multiple_of(odd * half, 8), half), :]
    theirs_ref[...] = part_ref[pl.ds(pl.multiple_of((1 - odd) * half, 8), half), :]


def join_halves(odd, full_ref, other_ref, joined_ref):
    half = full_ref.shape[0]
    joined_ref[pl.ds(pl.multiple_of(odd * half, 8), half), :] = full_ref[...]
    joined_ref[pl.ds(pl.multiple_of((1 - odd) * half, 8), half), :] = other_ref[...]


def norm_grad(upstream, normed, inverse):
    mean_grad = jnp.mean(upstream, axis=-1, keepdims=True)
    mean_proj = jnp.mean(upstream * normed, axis=-1, keepdims=True)
    return inverse * (upstream - mean_grad - normed * mean_proj)


def middle_back_kernel(
    odd_ref,
    full_ref,
    other_ref,
    attn_out_ref,
    hidden_ref,
    cotangent_ref,
    gate_ref,
    scale_ref,
    d_middle_ref,
    d_attn_ref,
    d_shift_ref,
    d_scale_ref,
    d_gate_ref,
    joined_ref,
):
    join_halves(odd_ref[0], full_ref, other_ref, joined_ref)
    for at, rows in enumerate(latent_rows(hidden_ref)):
        gate = gate_ref[at : at + 1, :]
        attn_out = attn_out_ref[rows, :]
        normed, inverse = of_rows(hidden_ref[rows, :].astype(F32) + gate * attn_out)
        d_mlp_in = joined_ref[rows, :]
        d_shift_ref[at : at + 1, :] = jnp.sum(d_mlp_in, axis=0, keepdims=True)
        d_scale_ref[at : at + 1, :] = jnp.sum(d_mlp_in * normed, axis=0, keepdims=True)
        d_middle = cotangent_ref[rows, :].astype(F32) + norm_grad(
            d_mlp_in * (1.0 + scale_ref[at : at + 1, :]), normed, inverse
        )
        d_middle_ref[rows, :] = d_middle
        d_gate_ref[at : at + 1, :] = jnp.sum(d_middle * attn_out, axis=0, keepdims=True)
        d_attn_ref[rows, :] = (d_middle * gate).astype(BF16)


def attention_back_kernel(
    odd_ref,
    d_attn_ref,
    mixing_ref,
    queries_ref,
    keys_ref,
    values_ref,
    weight_ref,
    d_queries_ref,
    d_keys_ref,
    d_values_ref,
    mine_ref,
    theirs_ref,
    part_ref,
):
    feats = queries_ref.shape[1]
    scale = HEAD_DIM ** (-0.5)
    for rows in latent_rows(d_attn_ref):
        d_attended = against_rows(d_attn_ref[rows, :], mixing_ref[...]).astype(BF16)
        queries, keys, values = queries_ref[rows, :], keys_ref[rows, :], values_ref[rows, :]
        d_queries, d_keys, d_values = [], [], []
        for cols in head_columns(feats):
            weights = softmax_rows(queries[:, cols], keys[:, cols])
            d_weights = against_rows(d_attended[:, cols], values[:, cols])
            row_dots = jnp.sum(weights * d_weights, axis=-1, keepdims=True)
            d_scores = (weights * (d_weights - row_dots)).astype(BF16)
            d_queries.append(times(d_scores, keys[:, cols]) * scale)
            d_keys.append(over_tokens(d_scores, queries[:, cols]) * scale)
            d_values.append(over_tokens(weights.astype(BF16), d_attended[:, cols]))
        total = None
        for at, (ref, columns) in enumerate(
            ((d_queries_ref, d_queries), (d_keys_ref, d_keys), (d_values_ref, d_values))
        ):
            joined = jnp.concatenate(columns, axis=1).astype(BF16)
            ref[rows, :] = joined
            term = times(joined, weight_ref[at * feats : (at + 1) * feats, :])
            total = term if total is None else total + term
        part_ref[rows, :] = total
    split_rows(odd_ref[0], part_ref, mine_ref, theirs_ref)


def input_back_kernel(
    odd_ref, full_ref, other_ref, hidden_ref, d_middle_ref, scale_ref, input_grad_ref, d_shift_ref, d_scale_ref, joined_ref
):
    join_halves(odd_ref[0], full_ref, other_ref, joined_ref)
    for at, rows in enumerate(latent_rows(hidden_ref)):
        normed, inverse = of_rows(hidden_ref[rows, :].astype(F32))
        d_heads_in = joined_ref[rows, :]
        d_shift_ref[at : at + 1, :] = jnp.sum(d_heads_in, axis=0, keepdims=True)
        d_scale_ref[at : at + 1, :] = jnp.sum(d_heads_in * normed, axis=0, keepdims=True)
        input_grad_ref[rows, :] = d_middle_ref[rows, :] + norm_grad(
            d_heads_in * (1.0 + scale_ref[at : at + 1, :]), normed, inverse
        )


def block_out_kernel(
    odd_ref,
    full_ref,
    other_ref,
    bias_ref,
    attn_out_ref,
    hidden_ref,
    cotangent_ref,
    gate_one_ref,
    gate_two_ref,
    block_out_ref,
    d_gate_ref,
    joined_ref,
):
    join_halves(odd_ref[0], full_ref, other_ref, joined_ref)
    for at, rows in enumerate(latent_rows(hidden_ref)):
        mlp_out = joined_ref[rows, :] + bias_ref[...].astype(F32)
        middle = hidden_ref[rows, :].astype(F32) + gate_one_ref[at : at + 1, :] * attn_out_ref[rows, :]
        block_out_ref[rows, :] = (middle + gate_two_ref[at : at + 1, :] * mlp_out).astype(BF16)
        d_gate_ref[at : at + 1, :] = jnp.sum(
            cotangent_ref[rows, :].astype(F32) * mlp_out, axis=0, keepdims=True
        )


def sum_kernel(left_ref, right_ref, out_ref):
    out_ref[...] = left_ref[...] + right_ref[...]


def modulation_grad_kernel(mods_ref, silu_ref, weight_ref, weight_grad_ref, bias_grad_ref, silu_grad_ref):
    mods = mods_ref[...].astype(BF16)
    weight_grad_ref[...] = lax.dot_general(
        silu_ref[...], mods, (((0,), (0,)), ((), ())), preferred_element_type=F32
    )
    bias_grad_ref[...] = jnp.sum(mods.astype(F32), axis=0, keepdims=True)
    silu_grad_ref[...] = lax.dot_general(
        mods, weight_ref[...], (((1,), (1,)), ((), ())), preferred_element_type=F32
    )


def after(values, gate):
    flat, tree = jax.tree.flatten(values)
    return jax.tree.unflatten(tree, lax.optimization_barrier((*flat, gate))[:-1])


def on_device(
    tensor_size,
    dp_size,
    hidden_in,
    out_cotangent,
    class_label,
    time_step,
    modulation_weight,
    modulation_bias,
    heads_weight,
    heads_bias,
    mixing_weight,
    mixing_bias,
    up_weight,
    up_bias,
    down_weight,
    down_bias,
    class_table,
    time_table,
):
    model_width = hidden_in.shape[1]
    own_latents = hidden_in.shape[0] // SEQ
    tok_rows = own_latents * SEQ
    lat_first = lax.axis_index("dp") * own_latents

    class_pick = jax.nn.one_hot(class_label, class_table.shape[0], dtype=BF16)
    time_pick = jax.nn.one_hot(time_step, time_table.shape[0], dtype=BF16)
    cond_part = jnp.dot(class_pick, class_table, preferred_element_type=F32) + jnp.dot(
        time_pick, time_table, preferred_element_type=F32
    )
    condition = join_columns(cond_part, tensor_size)
    silu_all = jax.nn.silu(condition).astype(BF16)
    silu_own = lax.dynamic_slice_in_dim(silu_all, lat_first, own_latents)
    mod_part = jnp.dot(silu_own, modulation_weight, preferred_element_type=F32) + modulation_bias.astype(F32)
    modulation = join_columns(mod_part, tensor_size)
    shift_one, scale_one, gate_one, shift_two, scale_two, gate_two = (
        modulation[:, number * model_width : (number + 1) * model_width] for number in range(6)
    )

    own_feats = heads_weight.shape[2]
    half = tok_rows // 2
    index = lax.axis_index("tensor")
    ways = (1, -1)
    table = ring_table(ways, dp_size)
    rings = whole_blocks((model_width, own_feats, up_weight.shape[1]), dp_size)
    flags = jnp.stack([index % 2, index // 2]).astype(jnp.int32)
    tokens = lambda dtype: jax.ShapeDtypeStruct((tok_rows, model_width), dtype)
    features = lambda dtype: jax.ShapeDtypeStruct((tok_rows, own_feats), dtype)
    halves = jax.ShapeDtypeStruct((half, model_width), F32)
    per_latent = jax.ShapeDtypeStruct((own_latents, model_width), F32)
    add = lambda left, right: call(sum_kernel, halves, (left, right), scalars=0, limit=SMALL_LIMIT)

    mixing_own = call(
        widen_kernel,
        jax.ShapeDtypeStruct(mixing_weight.shape, F32),
        (mixing_weight, gate_two),
        scalars=0,
        limit=SMALL_LIMIT,
    )
    bias_rows = [bias.reshape(1, bias.shape[0]) for bias in (mixing_bias, up_bias, down_bias)]
    heads_rows = heads_weight.transpose(1, 2, 0).reshape(3 * own_feats, model_width)
    heads_in, queries, key_rows, value_rows, attended = call(
        attend_kernel,
        (tokens(BF16), features(BF16), features(BF16), features(BF16), features(F32)),
        (table, flags, *bias_rows, hidden_in, scale_one, shift_one, heads_rows, heads_bias),
        scalars=2,
    )
    mixing_far = swap(mixing_own, tensor_size, 2)
    attended_across = swap(attended, tensor_size, 2)
    attended_beside = swap(attended, tensor_size, 1)
    d_mlp, d_act = call(
        cotangent_kernel,
        (tokens(BF16), jax.ShapeDtypeStruct((tok_rows, down_weight.shape[0]), F32)),
        (after(out_cotangent, attended), gate_two, down_weight),
        scalars=0,
    )
    attended_across = after(attended_across, d_act)
    mixing_across = after(mixing_far, attended_across)
    mixing_blocks = (
        mixing_own,
        swap(mixing_own, tensor_size, 1),
        mixing_across,
        swap(mixing_across, tensor_size, 1),
    )
    attn_out, mlp_in, activated, d_pre, mine, theirs = call(
        mlp_kernel,
        (
            tokens(F32),
            tokens(BF16),
            jax.ShapeDtypeStruct((tok_rows, up_weight.shape[1]), BF16),
            jax.ShapeDtypeStruct((tok_rows, up_weight.shape[1]), BF16),
            halves,
            halves,
        ),
        (
            flags,
            attended,
            attended_beside,
            attended_across,
            swap(attended_across, tensor_size, 1),
            *mixing_blocks,
            bias_rows[0],
            hidden_in,
            gate_one,
            scale_two,
            shift_two,
            up_weight,
            bias_rows[1],
            d_act,
        ),
        scratch=[pltpu.VMEM((tok_rows, model_width), F32)],
    )
    chip_two = add(mine, swap(theirs, tensor_size, 1))

    activated, d_pre = after((activated, d_pre), chip_two)
    up_part, down_part, mlp_bias, up_first, down_first, mine, theirs = call(
        mlp_grads_kernel,
        (
            jax.ShapeDtypeStruct((model_width, d_pre.shape[1]), F32),
            jax.ShapeDtypeStruct((activated.shape[1], model_width), F32),
            jax.ShapeDtypeStruct((2, model_width), F32),
            jax.ShapeDtypeStruct((model_width // dp_size, d_pre.shape[1]), F32),
            jax.ShapeDtypeStruct((activated.shape[1] // dp_size, model_width), F32),
            halves,
            halves,
        ),
        (table, flags, mlp_in, d_pre, activated, d_mlp, down_weight),
        scalars=2,
        scratch=[pltpu.VMEM((tok_rows, model_width), F32)],
    )
    mlp_ring = start_sum((up_part, down_part), (up_first, down_first), ways, dp_size, table, rings)
    chip_out = add(mine, swap(theirs, tensor_size, 1))
    mlp_ring.step()
    across_two = after(after(swap(chip_two, tensor_size, 2), chip_out), mlp_ring.step())
    full_two = add(chip_two, across_two)
    chip_out = after(chip_out, full_two)
    out_across = swap(chip_out, tensor_size, 2)
    d_middle, d_attn, d_shift_two, d_scale_two, d_gate_one = call(
        middle_back_kernel,
        (tokens(F32), tokens(BF16), per_latent, per_latent, per_latent),
        (
            flags,
            full_two,
            swap(full_two, tensor_size, 1),
            attn_out,
            hidden_in,
            out_cotangent,
            gate_one,
            scale_two,
        ),
        scratch=[pltpu.VMEM((tok_rows, model_width), F32)],
    )
    d_attn = after(d_attn, mlp_ring.step(d_attn))
    d_queries, d_keys, d_values, mine, theirs = call(
        attention_back_kernel,
        (features(BF16), features(BF16), features(BF16), halves, halves),
        (flags, d_attn, mixing_weight, queries, key_rows, value_rows, heads_rows),
        scratch=[pltpu.VMEM((tok_rows, model_width), F32)],
    )
    beside_one = after(swap(theirs, tensor_size, 1), mlp_ring.step(theirs))
    full_out = add(chip_out, out_across)
    chip_one = after(add(mine, beside_one), full_out)
    out_other = swap(full_out, tensor_size, 1)

    d_queries, d_keys, d_values = after((d_queries, d_keys, d_values), chip_one)
    blocks = dp_size if rings else 1
    upper_rows, lower_rows = 2 * own_feats, 2 * own_feats + 8 * dp_size
    upper_part, lower_part, upper_first, lower_first = call(
        functools.partial(attention_grads_kernel, blocks),
        (
            jax.ShapeDtypeStruct((upper_rows, model_width), F32),
            jax.ShapeDtypeStruct((lower_rows, model_width), F32),
            jax.ShapeDtypeStruct((upper_rows // dp_size, model_width), F32),
            jax.ShapeDtypeStruct((lower_rows // dp_size, model_width), F32),
        ),
        (table, heads_in, d_queries, d_keys, d_values, attended, d_attn, mlp_bias),
    )
    heads_ring = start_sum((upper_part, lower_part), (upper_first, lower_first), ways, dp_size, table, rings)
    block_out, d_gate_two = call(
        block_out_kernel,
        (jax.ShapeDtypeStruct((tok_rows, model_width), BF16), per_latent),
        (
            flags,
            full_out,
            after(out_other, upper_first),
            bias_rows[2],
            attn_out,
            hidden_in,
            out_cotangent,
            gate_one,
            gate_two,
        ),
        scratch=[pltpu.VMEM((tok_rows, model_width), F32)],
    )
    gate = mlp_ring.step(heads_ring.step(d_gate_two))
    across_one = after(swap(chip_one, tensor_size, 2), gate)
    full_one = add(chip_one, across_one)
    input_grad, d_shift_one, d_scale_one = call(
        input_back_kernel,
        (jax.ShapeDtypeStruct((tok_rows, model_width), F32), per_latent, per_latent),
        (
            flags,
            full_one,
            after(swap(full_one, tensor_size, 1), heads_ring.step(full_one)),
            hidden_in,
            d_middle,
            scale_one,
        ),
        scratch=[pltpu.VMEM((tok_rows, model_width), F32)],
    )
    d_modulation = jnp.concatenate(
        [d_shift_one, d_scale_one, d_gate_one, d_shift_two, d_scale_two, d_gate_two], axis=1
    )
    own_cols = modulation_weight.shape[1]
    own_mods = lax.dynamic_slice_in_dim(d_modulation, lax.axis_index("tensor") * own_cols, own_cols, 1)
    mlp_ring.step(own_mods)
    heads_ring.step(own_mods)
    whole = (1, 1)
    up_weight_sum, down_weight_sum = mlp_ring.finish(
        (((whole, 0),), ((whole, 1),)), (up_part.shape, down_part.shape)
    )
    run = (own_feats, lower_rows)
    heads_sum, mixing_weight_sum, bias_sum = heads_ring.finish(
        (((whole, 0),), ((run, 0), (run, 1), ((8 * dp_size, lower_rows), 2))),
        ((3 * own_feats, model_width), (own_feats, model_width), (8 * dp_size, model_width)),
    )
    heads_weight_sum = heads_sum.reshape(3, own_feats, model_width).transpose(2, 0, 1)
    up_bias_sum, down_bias_sum, mixing_bias_sum = (bias_sum[row] for row in range(3))
    heads_bias_sum = bias_sum[3:5, :own_feats]
    all_mods = gather_latents(own_mods, dp_size)
    mod_weight_sum, mod_bias_row, d_silu_part = call(
        modulation_grad_kernel,
        (
            jax.ShapeDtypeStruct((model_width, own_cols), F32),
            jax.ShapeDtypeStruct((1, own_cols), F32),
            jax.ShapeDtypeStruct((all_mods.shape[0], model_width), F32),
        ),
        (all_mods, silu_all, modulation_weight),
        scalars=0,
    )
    mod_bias_sum = mod_bias_row.reshape(own_cols)
    d_silu_own = scatter_features(d_silu_part, tensor_size)
    sigmoid_part = jax.nn.sigmoid(cond_part)
    d_condition = d_silu_own * sigmoid_part * (1.0 + cond_part * (1.0 - sigmoid_part))
    exact = dict(preferred_element_type=F32, precision=lax.Precision.HIGHEST)
    class_sum = jnp.einsum("lk,lf->kf", class_pick.astype(F32), d_condition, **exact)
    time_sum = jnp.einsum("lk,lf->kf", time_pick.astype(F32), d_condition, **exact)
    return (
        block_out,
        input_grad,
        mod_weight_sum,
        mod_bias_sum,
        heads_weight_sum,
        heads_bias_sum,
        mixing_weight_sum,
        mixing_bias_sum,
        up_weight_sum,
        up_bias_sum,
        down_weight_sum,
        down_bias_sum,
        class_sum,
        time_sum,
    )


def solution(mesh):
    in_specs = (
        P("dp", None),
        P("dp", None),
        P(),
        P(),
        P(None, "tensor"),
        P("tensor"),
        P(None, None, "tensor"),
        P(None, "tensor"),
        P("tensor", None),
        P(),
        P(None, "tensor"),
        P("tensor"),
        P("tensor", None),
        P(),
        P(None, "tensor"),
        P(None, "tensor"),
    )
    out_specs = (
        P("dp", None),
        P("dp", None),
        P(None, "tensor"),
        P("tensor"),
        P(None, None, "tensor"),
        P(None, "tensor"),
        P("tensor", None),
        P(),
        P(None, "tensor"),
        P("tensor"),
        P("tensor", None),
        P(),
        P(None, "tensor"),
        P(None, "tensor"),
    )

    def run(*args):
        return on_device(mesh.shape["tensor"], mesh.shape["dp"], *args)

    return jax.shard_map(run, mesh=mesh, in_specs=in_specs, out_specs=out_specs, check_vma=False)
```

```python
import functools
import math

import jax
import jax.numpy as jnp
from jax import lax
from jax.experimental import pallas as pl
from jax.experimental.pallas import tpu as pltpu
from jax.sharding import PartitionSpec as P

SEQ = 256
HEAD_DIM = 64
F32 = jnp.float32
BF16 = jnp.bfloat16


def swap(values, size, bit):
    return lax.ppermute(values, "tensor", [(at, at ^ bit) for at in range(size)])


def ring_place(size):
    order = list(range(0, size, 2)) + list(range(size - 1, 0, -2))
    index = lax.axis_index("dp")
    place = jnp.where(index % 2 == 0, index // 2, size - 1 - index // 2)
    return order, place


def gather_latents(own, size):
    if size % 2 or size > 16:
        return lax.all_gather(own, "dp", axis=0, tiled=True)
    rows = own.shape[0]
    index = lax.axis_index("dp")
    other = lax.ppermute(own, "dp", [(at, at ^ 1) for at in range(size)])
    odd = index % 2 == 1
    pair = jnp.concatenate([jnp.where(odd, other, own), jnp.where(odd, own, other)], axis=0)
    out = jnp.zeros((size * rows, own.shape[1]), own.dtype)
    out = lax.dynamic_update_slice_in_dim(out, pair, (index // 2) * 2 * rows, 0)
    for step in range(2, size, 2):
        got = lax.ppermute(pair, "dp", [(at, (at + step) % size) for at in range(size)])
        out = lax.dynamic_update_slice_in_dim(out, got, (((index - step) % size) // 2) * 2 * rows, 0)
    return out


def scatter_features(part, size):
    index = lax.axis_index("tensor")
    columns = part.shape[1] // size
    block = lambda at: lax.dynamic_slice_in_dim(part, at * columns, columns, 1)
    total = block(index)
    for bit in range(1, size):
        total = total + swap(block(index ^ bit), size, bit)
    return total


VMEM_LIMIT = 20 * 1024 * 1024
SMALL_LIMIT = 8 * 1024 * 1024
GELU_SCALE = (2.0 / math.pi) ** 0.5
IN_VMEM = pl.BlockSpec(memory_space=pltpu.VMEM)
IN_SMEM = pl.BlockSpec(memory_space=pltpu.SMEM)


QUICK = pl.CostEstimate(flops=1, transcendentals=0, bytes_accessed=1)


def call(kernel, out_shape, operands, scalars=1, scratch=(), limit=VMEM_LIMIT):
    single = not isinstance(out_shape, tuple)
    return pl.pallas_call(
        kernel,
        out_shape=out_shape,
        in_specs=[IN_SMEM] * scalars + [IN_VMEM] * (len(operands) - scalars),
        out_specs=IN_VMEM if single else [IN_VMEM] * len(out_shape),
        scratch_shapes=list(scratch),
        compiler_params=pltpu.CompilerParams(vmem_limit_bytes=limit),
        cost_estimate=QUICK,
    )(*operands)


def natural(blocks):
    index = lax.axis_index("tensor")
    low, high = index % 2 == 1, index >= 2
    return [
        jnp.where(
            high,
            jnp.where(low, blocks[at ^ 3], blocks[at ^ 2]),
            jnp.where(low, blocks[at ^ 1], blocks[at]),
        )
        for at in range(4)
    ]


def join_columns(own, size):
    blocks = [own] + [swap(own, size, bit) for bit in range(1, size)]
    return jnp.concatenate(natural(blocks), axis=1)


def place_kernel(steps, size, first, targets, outs, kept, spots_ref, *refs):
    count = len(targets)
    pieces = refs[: steps * count]
    out_refs = refs[steps * count + kept : steps * count + kept + outs]
    token_ref, sems = refs[-2], refs[-1]
    copies = []
    filled = [0] * outs
    for entry, runs in enumerate(targets):
        height = pieces[entry].shape[0]
        at = 0
        for share, out in runs:
            rows = height * share[0] // share[1]
            for step in range(steps):
                start = pl.multiple_of(spots_ref[first + step, entry] * rows + filled[out], 8)
                copies.append(
                    pltpu.make_async_copy(
                        pieces[step * count + entry].at[pl.ds(at, rows), :],
                        out_refs[out].at[pl.ds(start, rows), :],
                        sems.at[len(copies)],
                    )
                )
            at += rows
            filled[out] += rows * size
    for copy in copies:
        copy.start()
    token_ref[...] = jnp.zeros(token_ref.shape, F32)
    for copy in copies:
        copy.wait()


def place_rows(pieces, size, table, first, targets, shapes, filled=()):
    steps = len(pieces)
    copies = steps * sum(len(runs) for runs in targets)
    operands = [piece for step in pieces for piece in step]
    anywhere = pl.BlockSpec(memory_space=pl.ANY)
    *outs, token = pl.pallas_call(
        functools.partial(place_kernel, steps, size, first, targets, len(shapes), len(filled)),
        out_shape=[jax.ShapeDtypeStruct(shape, F32) for shape in (*shapes, (8, 128))],
        in_specs=[IN_SMEM] + [IN_VMEM] * len(operands) + [anywhere] * len(filled),
        out_specs=[anywhere] * len(shapes) + [IN_VMEM],
        scratch_shapes=[pltpu.SemaphoreType.DMA((copies,))],
        input_output_aliases={1 + len(operands) + at: at for at in range(len(filled))},
        compiler_params=pltpu.CompilerParams(vmem_limit_bytes=SMALL_LIMIT),
        cost_estimate=QUICK,
    )(table, *operands, *filled)
    return outs, token


def add_kernel(step, spots_ref, *refs):
    count = len(refs) // 3
    for at in range(count):
        moved_ref, part_ref, out_ref = refs[at], refs[count + at], refs[2 * count + at]
        rows = moved_ref.shape[0]
        start = pl.multiple_of(spots_ref[step, at] * rows, 8)
        out_ref[...] = moved_ref[...] + part_ref[pl.ds(start, rows), :]


def add_pieces(moving, parts, table, step):
    return call(
        functools.partial(add_kernel, step),
        tuple(jax.ShapeDtypeStruct(held.shape, F32) for held in moving),
        (table, *moving, *parts),
        limit=SMALL_LIMIT,
    )


def ring_table(ways, size):
    order, place = ring_place(size)
    steps = jnp.arange(2 * size - 1, dtype=jnp.int32)[:, None]
    return (place - jnp.asarray(ways, jnp.int32)[None, :] * steps) % size


class Ring:
    def __init__(self, parts, firsts, ways, size, table):
        order, place = ring_place(size)
        self.perms = [[(order[at], order[(at + way) % size]) for at in range(size)] for way in ways]
        self.table = table
        self.parts, self.size, self.count = parts, size, 0
        self.moving = list(firsts)
        self.pieces = []

    def step(self, gate=None):
        if self.count == 2 * self.size - 2:
            return self.moving[0]
        self.count += 1
        self.moving = [lax.ppermute(held, "dp", perm) for held, perm in zip(self.moving, self.perms)]
        if gate is not None:
            self.moving = after(self.moving, gate)
        if self.count < self.size:
            self.moving = add_pieces(self.moving, self.parts, self.table, self.count)
        if self.count >= self.size - 1:
            self.pieces.append(self.moving)
        return self.moving[0]

    def finish(self, targets, shapes, gate=None):
        steps = 2 * self.size - 2
        while self.count < steps - 2:
            self.step()
        early = len(self.pieces)
        outs, token = place_rows(self.pieces, self.size, self.table, self.size - 1, targets, shapes)
        self.step(token)
        if gate is not None:
            self.moving = after(self.moving, gate)
        self.step()
        return place_rows(
            self.pieces[early:], self.size, self.table, self.size - 1 + early, targets, shapes, outs
        )


class Plain:
    def __init__(self, parts):
        self.parts = parts

    def step(self, gate=None):
        return self.parts[0]

    def finish(self, targets, shapes, gate=None):
        outs = [[] for shape in shapes]
        for part, runs in zip(lax.psum(self.parts, "dp"), targets):
            at = 0
            for share, out in runs:
                rows = part.shape[0] * share[0] // share[1]
                outs[out].append(part[at : at + rows])
                at += rows
        return [jnp.concatenate(rows, axis=0) for rows in outs], None


def whole_blocks(heights, size):
    return size <= 16 and size % 2 == 0 and all(height % (8 * size) == 0 for height in heights)


def start_sum(parts, firsts, ways, size, table, rings):
    return Ring(parts, firsts, ways, size, table) if rings else Plain(parts)


def column_sums(values):
    return jnp.sum(values.astype(F32), axis=0, keepdims=True)


def over_tokens(left, right):
    return lax.dot_general(left, right, (((0,), (0,)), ((), ())), preferred_element_type=F32)


def copy_block(spots_ref, at, part_ref, first_ref):
    rows = first_ref.shape[0]
    first_ref[...] = part_ref[pl.ds(pl.multiple_of(spots_ref[0, at] * rows, 8), rows), :]


def mlp_grads_kernel(
    spots_ref,
    flags_ref,
    mlp_in_ref,
    d_pre_ref,
    activated_ref,
    d_mlp_ref,
    down_weight_ref,
    up_ref,
    down_ref,
    bias_ref,
    up_first_ref,
    down_first_ref,
    mine_ref,
    theirs_ref,
    part_ref,
):
    up_ref[...] = over_tokens(mlp_in_ref[...], d_pre_ref[...])
    down_ref[...] = over_tokens(activated_ref[...], d_mlp_ref[...])
    bias_ref[0:1, :] = column_sums(d_pre_ref[...])
    bias_ref[1:2, :] = column_sums(d_mlp_ref[...])
    copy_block(spots_ref, 0, up_ref, up_first_ref)
    copy_block(spots_ref, 1, down_ref, down_first_ref)
    part_ref[...] = jnp.dot(activated_ref[...], down_weight_ref[...], preferred_element_type=F32)
    split_rows(flags_ref[0], part_ref, mine_ref, theirs_ref)


def attention_grads_kernel(
    blocks,
    spots_ref,
    heads_in_ref,
    d_queries_ref,
    d_keys_ref,
    d_values_ref,
    attended_ref,
    d_attn_ref,
    upper_ref,
    lower_ref,
    upper_first_ref,
    lower_first_ref,
    bias_ref,
):
    feats = d_queries_ref.shape[1]
    heads_in = heads_in_ref[...]
    upper_ref[0:feats, :] = over_tokens(d_queries_ref[...], heads_in)
    upper_ref[feats : 2 * feats, :] = over_tokens(d_keys_ref[...], heads_in)
    values_part = over_tokens(d_values_ref[...], heads_in)
    mixing_part = over_tokens(attended_ref[...].astype(BF16), d_attn_ref[...])
    run = feats // blocks
    for at in range(blocks):
        base = at * 2 * run
        lower_ref[base : base + run, :] = values_part[at * run : (at + 1) * run]
        lower_ref[base + run : base + 2 * run, :] = mixing_part[at * run : (at + 1) * run]
    bias_ref[...] = jnp.zeros(bias_ref.shape, F32)
    bias_ref[0:1, :] = column_sums(d_attn_ref[...])
    bias_ref[1:2, 0:feats] = column_sums(d_queries_ref[...])
    bias_ref[2:3, 0:feats] = column_sums(d_values_ref[...])
    copy_block(spots_ref, 0, upper_ref, upper_first_ref)
    copy_block(spots_ref, 1, lower_ref, lower_first_ref)


def of_rows(values):
    centered = values - jnp.mean(values, axis=-1, keepdims=True)
    inverse = lax.rsqrt(jnp.mean(centered * centered, axis=-1, keepdims=True) + 1e-06)
    return centered * inverse, inverse


def against_rows(left, right):
    return lax.dot_general(left, right, (((1,), (1,)), ((), ())), preferred_element_type=F32)


def times(left, right):
    return jnp.dot(left, right, preferred_element_type=F32)


def latent_rows(ref):
    return [slice(at * SEQ, (at + 1) * SEQ) for at in range(ref.shape[0] // SEQ)]


def head_columns(columns):
    return [slice(at * HEAD_DIM, (at + 1) * HEAD_DIM) for at in range(columns // HEAD_DIM)]


def softmax_rows(queries, key_rows):
    scores = against_rows(queries, key_rows) * HEAD_DIM ** (-0.5)
    exp_terms = jnp.exp(scores - jnp.max(scores, axis=-1, keepdims=True))
    return exp_terms / jnp.sum(exp_terms, axis=-1, keepdims=True)


def attend_kernel(
    table_ref, flags_ref, mixing_bias_ref, up_bias_ref, down_bias_ref, hidden_ref, scale_ref, shift_ref, weight_ref, bias_ref, heads_in_ref, queries_ref, keys_ref, values_ref, attended_ref
):
    feats = queries_ref.shape[1]
    bias = bias_ref[...].astype(F32)
    for at, rows in enumerate(latent_rows(hidden_ref)):
        normed, inverse = of_rows(hidden_ref[rows, :].astype(F32))
        heads_in = (normed * (1.0 + scale_ref[at : at + 1, :]) + shift_ref[at : at + 1, :]).astype(BF16)
        heads_in_ref[rows, :] = heads_in
        queries = (against_rows(heads_in, weight_ref[0:feats, :]) + bias[0:1]).astype(BF16)
        keys = against_rows(heads_in, weight_ref[feats : 2 * feats, :]).astype(BF16)
        values = (against_rows(heads_in, weight_ref[2 * feats : 3 * feats, :]) + bias[1:2]).astype(BF16)
        queries_ref[rows, :] = queries
        keys_ref[rows, :] = keys
        values_ref[rows, :] = values
        mixed = []
        for cols in head_columns(feats):
            weights = softmax_rows(queries[:, cols], keys[:, cols])
            mixed.append(times(weights.astype(BF16), values[:, cols]))
        attended_ref[rows, :] = jnp.concatenate(mixed, axis=1).astype(BF16).astype(F32)


def in_order(flags_ref, blocks):
    low, high = flags_ref[0] == 1, flags_ref[1] == 1
    return [
        jnp.where(
            high,
            jnp.where(low, blocks[at ^ 3], blocks[at ^ 2]),
            jnp.where(low, blocks[at ^ 1], blocks[at]),
        )
        for at in range(4)
    ]


def widen_kernel(first, values_ref, behind_ref, out_ref):
    out_ref[...] = values_ref[first : first + out_ref.shape[0], :].astype(F32)


def cotangent_kernel(cotangent_ref, gate_ref, down_ref, d_mlp_ref, d_act_ref):
    for at, rows in enumerate(latent_rows(cotangent_ref)):
        d_mlp = (cotangent_ref[rows, :].astype(F32) * gate_ref[at : at + 1, :]).astype(BF16)
        d_mlp_ref[rows, :] = d_mlp
        d_act_ref[rows, :] = against_rows(d_mlp, down_ref[...])


def mlp_kernel(
    odd_ref,
    own_ref,
    beside_ref,
    across_ref,
    corner_ref,
    mixing_0_ref,
    mixing_1_ref,
    mixing_2_ref,
    mixing_3_ref,
    mixing_4_ref,
    mixing_5_ref,
    mixing_6_ref,
    mixing_7_ref,
    mixing_bias_ref,
    hidden_ref,
    gate_ref,
    scale_ref,
    shift_ref,
    up_ref,
    up_bias_ref,
    d_act_ref,
    attn_out_ref,
    mlp_in_ref,
    activated_ref,
    d_pre_ref,
    mine_ref,
    theirs_ref,
    part_ref,
):
    odd = odd_ref[0]
    blocks = (own_ref, beside_ref, across_ref, corner_ref)
    mixing = in_order(
        odd_ref,
        [
            jnp.concatenate([top[...].astype(BF16), low[...].astype(BF16)], axis=0)
            for top, low in (
                (mixing_0_ref, mixing_1_ref),
                (mixing_2_ref, mixing_3_ref),
                (mixing_4_ref, mixing_5_ref),
                (mixing_6_ref, mixing_7_ref),
            )
        ],
    )
    for at, rows in enumerate(latent_rows(hidden_ref)):
        attn_out = mixing_bias_ref[...].astype(F32)
        for block, piece in enumerate(in_order(odd_ref, [ref[rows, :] for ref in blocks])):
            attn_out = attn_out + times(piece.astype(BF16), mixing[block])
        attn_out_ref[rows, :] = attn_out
        middle = hidden_ref[rows, :].astype(F32) + gate_ref[at : at + 1, :] * attn_out
        normed, inverse = of_rows(middle)
        mlp_in = (normed * (1.0 + scale_ref[at : at + 1, :]) + shift_ref[at : at + 1, :]).astype(BF16)
        mlp_in_ref[rows, :] = mlp_in
        pre_act = times(mlp_in, up_ref[...]) + up_bias_ref[...].astype(F32)
        square = pre_act * pre_act
        bend = jnp.tanh(GELU_SCALE * pre_act * (1.0 + 0.044715 * square))
        activated_ref[rows, :] = (0.5 * pre_act * (1.0 + bend)).astype(BF16)
        slope = 0.5 * (1.0 + bend) + 0.5 * pre_act * (1.0 - bend * bend) * (
            GELU_SCALE * (1.0 + 3.0 * 0.044715 * square)
        )
        d_pre = (d_act_ref[rows, :] * slope).astype(BF16)
        d_pre_ref[rows, :] = d_pre
        part_ref[rows, :] = against_rows(d_pre, up_ref[...])
    split_rows(odd, part_ref, mine_ref, theirs_ref)


def split_rows(odd, part_ref, mine_ref, theirs_ref):
    half = mine_ref.shape[0]
    mine_ref[...] = part_ref[pl.ds(pl.multiple_of(odd * half, 8), half), :]
    theirs_ref[...] = part_ref[pl.ds(pl.multiple_of((1 - odd) * half, 8), half), :]


def join_halves(odd, full_ref, other_ref, joined_ref):
    half = full_ref.shape[0]
    joined_ref[pl.ds(pl.multiple_of(odd * half, 8), half), :] = full_ref[...]
    joined_ref[pl.ds(pl.multiple_of((1 - odd) * half, 8), half), :] = other_ref[...]


def norm_grad(upstream, normed, inverse):
    mean_grad = jnp.mean(upstream, axis=-1, keepdims=True)
    mean_proj = jnp.mean(upstream * normed, axis=-1, keepdims=True)
    return inverse * (upstream - mean_grad - normed * mean_proj)


def middle_back_kernel(
    odd_ref,
    full_ref,
    other_ref,
    attn_out_ref,
    hidden_ref,
    cotangent_ref,
    gate_ref,
    scale_ref,
    d_middle_ref,
    d_attn_ref,
    d_shift_ref,
    d_scale_ref,
    d_gate_ref,
    joined_ref,
):
    join_halves(odd_ref[0], full_ref, other_ref, joined_ref)
    for at, rows in enumerate(latent_rows(hidden_ref)):
        gate = gate_ref[at : at + 1, :]
        attn_out = attn_out_ref[rows, :]
        normed, inverse = of_rows(hidden_ref[rows, :].astype(F32) + gate * attn_out)
        d_mlp_in = joined_ref[rows, :]
        d_shift_ref[at : at + 1, :] = jnp.sum(d_mlp_in, axis=0, keepdims=True)
        d_scale_ref[at : at + 1, :] = jnp.sum(d_mlp_in * normed, axis=0, keepdims=True)
        d_middle = cotangent_ref[rows, :].astype(F32) + norm_grad(
            d_mlp_in * (1.0 + scale_ref[at : at + 1, :]), normed, inverse
        )
        d_middle_ref[rows, :] = d_middle
        d_gate_ref[at : at + 1, :] = jnp.sum(d_middle * attn_out, axis=0, keepdims=True)
        d_attn_ref[rows, :] = (d_middle * gate).astype(BF16)


def attention_back_kernel(
    odd_ref,
    d_attn_ref,
    mixing_ref,
    queries_ref,
    keys_ref,
    values_ref,
    weight_ref,
    d_queries_ref,
    d_keys_ref,
    d_values_ref,
    mine_ref,
    theirs_ref,
    part_ref,
):
    feats = queries_ref.shape[1]
    scale = HEAD_DIM ** (-0.5)
    for rows in latent_rows(d_attn_ref):
        d_attended = against_rows(d_attn_ref[rows, :], mixing_ref[...]).astype(BF16)
        queries, keys, values = queries_ref[rows, :], keys_ref[rows, :], values_ref[rows, :]
        d_queries, d_keys, d_values = [], [], []
        for cols in head_columns(feats):
            weights = softmax_rows(queries[:, cols], keys[:, cols])
            d_weights = against_rows(d_attended[:, cols], values[:, cols])
            row_dots = jnp.sum(weights * d_weights, axis=-1, keepdims=True)
            d_scores = (weights * (d_weights - row_dots)).astype(BF16)
            d_queries.append(times(d_scores, keys[:, cols]) * scale)
            d_keys.append(over_tokens(d_scores, queries[:, cols]) * scale)
            d_values.append(over_tokens(weights.astype(BF16), d_attended[:, cols]))
        total = None
        for at, (ref, columns) in enumerate(
            ((d_queries_ref, d_queries), (d_keys_ref, d_keys), (d_values_ref, d_values))
        ):
            joined = jnp.concatenate(columns, axis=1).astype(BF16)
            ref[rows, :] = joined
            term = times(joined, weight_ref[at * feats : (at + 1) * feats, :])
            total = term if total is None else total + term
        part_ref[rows, :] = total
    split_rows(odd_ref[0], part_ref, mine_ref, theirs_ref)


def input_back_kernel(
    odd_ref, full_ref, other_ref, hidden_ref, d_middle_ref, scale_ref, input_grad_ref, d_shift_ref, d_scale_ref, joined_ref
):
    join_halves(odd_ref[0], full_ref, other_ref, joined_ref)
    for at, rows in enumerate(latent_rows(hidden_ref)):
        normed, inverse = of_rows(hidden_ref[rows, :].astype(F32))
        d_heads_in = joined_ref[rows, :]
        d_shift_ref[at : at + 1, :] = jnp.sum(d_heads_in, axis=0, keepdims=True)
        d_scale_ref[at : at + 1, :] = jnp.sum(d_heads_in * normed, axis=0, keepdims=True)
        input_grad_ref[rows, :] = d_middle_ref[rows, :] + norm_grad(
            d_heads_in * (1.0 + scale_ref[at : at + 1, :]), normed, inverse
        )


def block_out_kernel(
    odd_ref,
    full_ref,
    other_ref,
    bias_ref,
    attn_out_ref,
    hidden_ref,
    cotangent_ref,
    gate_one_ref,
    gate_two_ref,
    block_out_ref,
    d_gate_ref,
    joined_ref,
):
    join_halves(odd_ref[0], full_ref, other_ref, joined_ref)
    for at, rows in enumerate(latent_rows(hidden_ref)):
        mlp_out = joined_ref[rows, :] + bias_ref[...].astype(F32)
        middle = hidden_ref[rows, :].astype(F32) + gate_one_ref[at : at + 1, :] * attn_out_ref[rows, :]
        block_out_ref[rows, :] = (middle + gate_two_ref[at : at + 1, :] * mlp_out).astype(BF16)
        d_gate_ref[at : at + 1, :] = jnp.sum(
            cotangent_ref[rows, :].astype(F32) * mlp_out, axis=0, keepdims=True
        )


def sum_kernel(left_ref, right_ref, out_ref):
    out_ref[...] = left_ref[...] + right_ref[...]


def pack_kernel(
    flags_ref, shift_one, scale_one, gate_one, shift_two, scale_two, gate_two, mlp_bias_ref, heads_bias_ref, out_ref, all_ref
):
    latents, width = shift_one.shape
    columns = out_ref.shape[1]
    for at, ref in enumerate((shift_one, scale_one, gate_one, shift_two, scale_two, gate_two)):
        all_ref[:, at * width : (at + 1) * width] = ref[...]
    start = pl.multiple_of((flags_ref[0] + 2 * flags_ref[1]) * columns, 128)
    out_ref[...] = jnp.zeros(out_ref.shape, F32)
    out_ref[0:latents, :] = all_ref[:, pl.ds(start, columns)]
    out_ref[latents : latents + 2, 0:width] = mlp_bias_ref[...]
    out_ref[latents + 2 : latents + 5, 0:width] = heads_bias_ref[...]


def modulation_grad_kernel(
    latents, carried_ref, silu_ref, weight_ref, weight_grad_ref, bias_grad_ref, silu_grad_ref, bias_sum_ref
):
    groups = silu_ref.shape[0] // latents
    height = carried_ref.shape[0] // groups
    mods = jnp.concatenate(
        [carried_ref[at * height : at * height + latents, :] for at in range(groups)], axis=0
    ).astype(BF16)
    total = carried_ref[latents : latents + 5, :]
    for at in range(1, groups):
        total = total + carried_ref[at * height + latents : at * height + latents + 5, :]
    bias_sum_ref[...] = total
    weight_grad_ref[...] = lax.dot_general(
        silu_ref[...], mods, (((0,), (0,)), ((), ())), preferred_element_type=F32
    )
    bias_grad_ref[...] = jnp.sum(mods.astype(F32), axis=0, keepdims=True)
    silu_grad_ref[...] = lax.dot_general(
        mods, weight_ref[...], (((1,), (1,)), ((), ())), preferred_element_type=F32
    )


def after(values, gate):
    flat, tree = jax.tree.flatten(values)
    return jax.tree.unflatten(tree, lax.optimization_barrier((*flat, gate))[:-1])


def on_device(
    tensor_size,
    dp_size,
    hidden_in,
    out_cotangent,
    class_label,
    time_step,
    modulation_weight,
    modulation_bias,
    heads_weight,
    heads_bias,
    mixing_weight,
    mixing_bias,
    up_weight,
    up_bias,
    down_weight,
    down_bias,
    class_table,
    time_table,
):
    model_width = hidden_in.shape[1]
    own_latents = hidden_in.shape[0] // SEQ
    tok_rows = own_latents * SEQ
    lat_first = lax.axis_index("dp") * own_latents

    class_pick = jax.nn.one_hot(class_label, class_table.shape[0], dtype=BF16)
    time_pick = jax.nn.one_hot(time_step, time_table.shape[0], dtype=BF16)
    cond_part = jnp.dot(class_pick, class_table, preferred_element_type=F32) + jnp.dot(
        time_pick, time_table, preferred_element_type=F32
    )
    condition = join_columns(cond_part, tensor_size)
    silu_all = jax.nn.silu(condition).astype(BF16)
    silu_own = lax.dynamic_slice_in_dim(silu_all, lat_first, own_latents)
    mod_part = jnp.dot(silu_own, modulation_weight, preferred_element_type=F32) + modulation_bias.astype(F32)
    modulation = join_columns(mod_part, tensor_size)
    shift_one, scale_one, gate_one, shift_two, scale_two, gate_two = (
        modulation[:, number * model_width : (number + 1) * model_width] for number in range(6)
    )

    own_feats = heads_weight.shape[2]
    half = tok_rows // 2
    index = lax.axis_index("tensor")
    ways = (1, -1)
    table = ring_table(ways, dp_size)
    rings = whole_blocks((model_width, own_feats, up_weight.shape[1]), dp_size)
    flags = jnp.stack([index % 2, index // 2]).astype(jnp.int32)
    tokens = lambda dtype: jax.ShapeDtypeStruct((tok_rows, model_width), dtype)
    features = lambda dtype: jax.ShapeDtypeStruct((tok_rows, own_feats), dtype)
    halves = jax.ShapeDtypeStruct((half, model_width), F32)
    per_latent = jax.ShapeDtypeStruct((own_latents, model_width), F32)
    add = lambda left, right: call(sum_kernel, halves, (left, right), scalars=0, limit=SMALL_LIMIT)

    mixing_half = own_feats // 2
    mixing_own = [
        call(
            functools.partial(widen_kernel, first),
            jax.ShapeDtypeStruct((mixing_half, model_width), F32),
            (mixing_weight, behind),
            scalars=0,
            limit=SMALL_LIMIT,
        )
        for first, behind in ((0, cond_part), (mixing_half, gate_two))
    ]
    bias_rows = [bias.reshape(1, bias.shape[0]) for bias in (mixing_bias, up_bias, down_bias)]
    heads_rows = heads_weight.transpose(1, 2, 0).reshape(3 * own_feats, model_width)
    heads_in, queries, key_rows, value_rows, attended = call(
        attend_kernel,
        (tokens(BF16), features(BF16), features(BF16), features(BF16), features(F32)),
        (table, flags, *bias_rows, hidden_in, scale_one, shift_one, heads_rows, heads_bias),
        scalars=2,
    )
    mixing_far = [swap(rows, tensor_size, 2) for rows in mixing_own]
    attended_across = swap(attended, tensor_size, 2)
    attended_beside = swap(attended, tensor_size, 1)
    d_mlp, d_act = call(
        cotangent_kernel,
        (tokens(BF16), jax.ShapeDtypeStruct((tok_rows, down_weight.shape[0]), F32)),
        (after(out_cotangent, attended), gate_two, down_weight),
        scalars=0,
    )
    attended_across = after(attended_across, d_act)
    mixing_across = after(mixing_far, attended_across)
    mixing_blocks = (
        *mixing_own,
        *(swap(rows, tensor_size, 1) for rows in mixing_own),
        *mixing_across,
        *(swap(rows, tensor_size, 1) for rows in mixing_across),
    )
    attn_out, mlp_in, activated, d_pre, mine, theirs = call(
        mlp_kernel,
        (
            tokens(F32),
            tokens(BF16),
            jax.ShapeDtypeStruct((tok_rows, up_weight.shape[1]), BF16),
            jax.ShapeDtypeStruct((tok_rows, up_weight.shape[1]), BF16),
            halves,
            halves,
        ),
        (
            flags,
            attended,
            attended_beside,
            attended_across,
            swap(attended_across, tensor_size, 1),
            *mixing_blocks,
            bias_rows[0],
            hidden_in,
            gate_one,
            scale_two,
            shift_two,
            up_weight,
            bias_rows[1],
            d_act,
        ),
        scratch=[pltpu.VMEM((tok_rows, model_width), F32)],
    )
    chip_two = add(mine, swap(theirs, tensor_size, 1))

    activated, d_pre = after((activated, d_pre), chip_two)
    up_part, down_part, mlp_bias, up_first, down_first, mine, theirs = call(
        mlp_grads_kernel,
        (
            jax.ShapeDtypeStruct((model_width, d_pre.shape[1]), F32),
            jax.ShapeDtypeStruct((activated.shape[1], model_width), F32),
            jax.ShapeDtypeStruct((2, model_width), F32),
            jax.ShapeDtypeStruct((model_width // dp_size, d_pre.shape[1]), F32),
            jax.ShapeDtypeStruct((activated.shape[1] // dp_size, model_width), F32),
            halves,
            halves,
        ),
        (table, flags, mlp_in, d_pre, activated, d_mlp, down_weight),
        scalars=2,
        scratch=[pltpu.VMEM((tok_rows, model_width), F32)],
    )
    mlp_ring = start_sum((up_part, down_part), (up_first, down_first), ways, dp_size, table, rings)
    chip_out = add(mine, swap(theirs, tensor_size, 1))
    mlp_ring.step()
    across_two = after(after(swap(chip_two, tensor_size, 2), chip_out), mlp_ring.step())
    full_two = add(chip_two, across_two)
    chip_out = after(chip_out, full_two)
    out_across = swap(chip_out, tensor_size, 2)
    d_middle, d_attn, d_shift_two, d_scale_two, d_gate_one = call(
        middle_back_kernel,
        (tokens(F32), tokens(BF16), per_latent, per_latent, per_latent),
        (
            flags,
            full_two,
            swap(full_two, tensor_size, 1),
            attn_out,
            hidden_in,
            out_cotangent,
            gate_one,
            scale_two,
        ),
        scratch=[pltpu.VMEM((tok_rows, model_width), F32)],
    )
    d_attn = after(d_attn, mlp_ring.step(d_attn))
    d_queries, d_keys, d_values, mine, theirs = call(
        attention_back_kernel,
        (features(BF16), features(BF16), features(BF16), halves, halves),
        (flags, d_attn, mixing_weight, queries, key_rows, value_rows, heads_rows),
        scratch=[pltpu.VMEM((tok_rows, model_width), F32)],
    )
    beside_one = after(swap(theirs, tensor_size, 1), mlp_ring.step(theirs))
    full_out = add(chip_out, out_across)
    chip_one = after(add(mine, beside_one), full_out)
    out_other = swap(full_out, tensor_size, 1)

    d_queries, d_keys, d_values = after((d_queries, d_keys, d_values), chip_one)
    blocks = dp_size if rings else 1
    upper_rows, lower_rows = 2 * own_feats, 2 * own_feats
    upper_part, lower_part, upper_first, lower_first, heads_bias_part = call(
        functools.partial(attention_grads_kernel, blocks),
        (
            jax.ShapeDtypeStruct((upper_rows, model_width), F32),
            jax.ShapeDtypeStruct((lower_rows, model_width), F32),
            jax.ShapeDtypeStruct((upper_rows // dp_size, model_width), F32),
            jax.ShapeDtypeStruct((lower_rows // dp_size, model_width), F32),
            jax.ShapeDtypeStruct((3, model_width), F32),
        ),
        (table, heads_in, d_queries, d_keys, d_values, attended, d_attn),
    )
    heads_ring = start_sum((upper_part, lower_part), (upper_first, lower_first), ways, dp_size, table, rings)
    block_out, d_gate_two = call(
        block_out_kernel,
        (jax.ShapeDtypeStruct((tok_rows, model_width), BF16), per_latent),
        (
            flags,
            full_out,
            after(out_other, upper_first),
            bias_rows[2],
            attn_out,
            hidden_in,
            out_cotangent,
            gate_one,
            gate_two,
        ),
        scratch=[pltpu.VMEM((tok_rows, model_width), F32)],
    )
    gate = mlp_ring.step(heads_ring.step(d_gate_two))
    across_one = after(swap(chip_one, tensor_size, 2), gate)
    full_one = add(chip_one, across_one)
    input_grad, d_shift_one, d_scale_one = call(
        input_back_kernel,
        (jax.ShapeDtypeStruct((tok_rows, model_width), F32), per_latent, per_latent),
        (
            flags,
            full_one,
            swap(full_one, tensor_size, 1),
            hidden_in,
            d_middle,
            scale_one,
        ),
        scratch=[pltpu.VMEM((tok_rows, model_width), F32)],
    )
    own_cols = modulation_weight.shape[1]
    carried = -(-(own_latents + 5) // 8) * 8
    own_mods = call(
        pack_kernel,
        jax.ShapeDtypeStruct((carried, own_cols), F32),
        (
            flags,
            d_shift_one,
            d_scale_one,
            d_gate_one,
            d_shift_two,
            d_scale_two,
            d_gate_two,
            mlp_bias,
            heads_bias_part,
        ),
        scratch=[pltpu.VMEM((own_latents, 6 * model_width), F32)],
        limit=SMALL_LIMIT,
    )
    mlp_ring.step(own_mods)
    heads_ring.step(own_mods)
    whole = (1, 1)
    run = (1, 2)
    (heads_sum, mixing_weight_sum), placed = heads_ring.finish(
        (((whole, 0),), ((run, 0), (run, 1))),
        ((3 * own_feats, model_width), (own_feats, model_width)),
    )
    (up_weight_sum, down_weight_sum), placed = mlp_ring.finish(
        (((whole, 0),), ((whole, 1),)), (up_part.shape, down_part.shape), placed
    )
    heads_weight_sum = heads_sum.reshape(3, own_feats, model_width).transpose(2, 0, 1)
    all_mods = gather_latents(own_mods, dp_size)
    mod_weight_sum, mod_bias_row, d_silu_part, bias_sum = call(
        functools.partial(modulation_grad_kernel, own_latents),
        (
            jax.ShapeDtypeStruct((model_width, own_cols), F32),
            jax.ShapeDtypeStruct((1, own_cols), F32),
            jax.ShapeDtypeStruct((silu_all.shape[0], model_width), F32),
            jax.ShapeDtypeStruct((5, own_cols), F32),
        ),
        (all_mods, silu_all, modulation_weight),
        scalars=0,
    )
    mod_bias_sum = mod_bias_row.reshape(own_cols)
    up_bias_sum, down_bias_sum, mixing_bias_sum = (bias_sum[row, :model_width] for row in range(3))
    heads_bias_sum = bias_sum[3:5, :own_feats]
    d_silu_own = scatter_features(d_silu_part, tensor_size)
    sigmoid_part = jax.nn.sigmoid(cond_part)
    d_condition = d_silu_own * sigmoid_part * (1.0 + cond_part * (1.0 - sigmoid_part))
    exact = dict(preferred_element_type=F32, precision=lax.Precision.HIGHEST)
    class_sum = jnp.einsum("lk,lf->kf", class_pick.astype(F32), d_condition, **exact)
    time_sum = jnp.einsum("lk,lf->kf", time_pick.astype(F32), d_condition, **exact)
    return (
        block_out,
        input_grad,
        mod_weight_sum,
        mod_bias_sum,
        heads_weight_sum,
        heads_bias_sum,
        mixing_weight_sum,
        mixing_bias_sum,
        up_weight_sum,
        up_bias_sum,
        down_weight_sum,
        down_bias_sum,
        class_sum,
        time_sum,
    )


def solution(mesh):
    in_specs = (
        P("dp", None),
        P("dp", None),
        P(),
        P(),
        P(None, "tensor"),
        P("tensor"),
        P(None, None, "tensor"),
        P(None, "tensor"),
        P("tensor", None),
        P(),
        P(None, "tensor"),
        P("tensor"),
        P("tensor", None),
        P(),
        P(None, "tensor"),
        P(None, "tensor"),
    )
    out_specs = (
        P("dp", None),
        P("dp", None),
        P(None, "tensor"),
        P("tensor"),
        P(None, None, "tensor"),
        P(None, "tensor"),
        P("tensor", None),
        P(),
        P(None, "tensor"),
        P("tensor"),
        P("tensor", None),
        P(),
        P(None, "tensor"),
        P(None, "tensor"),
    )

    def run(*args):
        return on_device(mesh.shape["tensor"], mesh.shape["dp"], *args)

    return jax.shard_map(run, mesh=mesh, in_specs=in_specs, out_specs=out_specs, check_vma=False)
```

```python
import functools
import math

import jax
import jax.numpy as jnp
from jax import lax
from jax.experimental import pallas as pl
from jax.experimental.pallas import tpu as pltpu
from jax.sharding import PartitionSpec as P

SEQ = 256
HEAD_DIM = 64
F32 = jnp.float32
BF16 = jnp.bfloat16


def swap(values, size, bit):
    return lax.ppermute(values, "tensor", [(at, at ^ bit) for at in range(size)])


def ring_place(size):
    order = list(range(0, size, 2)) + list(range(size - 1, 0, -2))
    index = lax.axis_index("dp")
    place = jnp.where(index % 2 == 0, index // 2, size - 1 - index // 2)
    return order, place


def gather_latents(own, size):
    if size % 2 or size > 16:
        return lax.all_gather(own, "dp", axis=0, tiled=True)
    rows = own.shape[0]
    index = lax.axis_index("dp")
    other = lax.ppermute(own, "dp", [(at, at ^ 1) for at in range(size)])
    odd = index % 2 == 1
    pair = jnp.concatenate([jnp.where(odd, other, own), jnp.where(odd, own, other)], axis=0)
    out = jnp.zeros((size * rows, own.shape[1]), own.dtype)
    out = lax.dynamic_update_slice_in_dim(out, pair, (index // 2) * 2 * rows, 0)
    for step in range(2, size, 2):
        got = lax.ppermute(pair, "dp", [(at, (at + step) % size) for at in range(size)])
        out = lax.dynamic_update_slice_in_dim(out, got, (((index - step) % size) // 2) * 2 * rows, 0)
    return out


def scatter_features(part, size):
    index = lax.axis_index("tensor")
    columns = part.shape[1] // size
    block = lambda at: lax.dynamic_slice_in_dim(part, at * columns, columns, 1)
    total = block(index)
    for bit in range(1, size):
        total = total + swap(block(index ^ bit), size, bit)
    return total


VMEM_LIMIT = 20 * 1024 * 1024
SMALL_LIMIT = 8 * 1024 * 1024
GELU_SCALE = (2.0 / math.pi) ** 0.5
IN_VMEM = pl.BlockSpec(memory_space=pltpu.VMEM)
IN_SMEM = pl.BlockSpec(memory_space=pltpu.SMEM)


QUICK = pl.CostEstimate(flops=1, transcendentals=0, bytes_accessed=1)


def call(kernel, out_shape, operands, scalars=1, scratch=(), limit=VMEM_LIMIT):
    single = not isinstance(out_shape, tuple)
    return pl.pallas_call(
        kernel,
        out_shape=out_shape,
        in_specs=[IN_SMEM] * scalars + [IN_VMEM] * (len(operands) - scalars),
        out_specs=IN_VMEM if single else [IN_VMEM] * len(out_shape),
        scratch_shapes=list(scratch),
        compiler_params=pltpu.CompilerParams(vmem_limit_bytes=limit),
        cost_estimate=QUICK,
    )(*operands)


def natural(blocks):
    index = lax.axis_index("tensor")
    low, high = index % 2 == 1, index >= 2
    return [
        jnp.where(
            high,
            jnp.where(low, blocks[at ^ 3], blocks[at ^ 2]),
            jnp.where(low, blocks[at ^ 1], blocks[at]),
        )
        for at in range(4)
    ]


def join_columns(own, size):
    blocks = [own] + [swap(own, size, bit) for bit in range(1, size)]
    return jnp.concatenate(natural(blocks), axis=1)


def place_kernel(steps, size, first, targets, outs, kept, waits, spots_ref, *refs):
    refs = refs[waits:]
    count = len(targets)
    pieces = refs[: steps * count]
    out_refs = refs[steps * count + kept : steps * count + kept + outs]
    token_ref, sems = refs[-2], refs[-1]
    copies = []
    filled = [0] * outs
    for entry, runs in enumerate(targets):
        height = pieces[entry].shape[0]
        at = 0
        for share, out in runs:
            rows = height * share[0] // share[1]
            for step in range(steps):
                start = pl.multiple_of(spots_ref[first + step, entry] * rows + filled[out], 8)
                copies.append(
                    pltpu.make_async_copy(
                        pieces[step * count + entry].at[pl.ds(at, rows), :],
                        out_refs[out].at[pl.ds(start, rows), :],
                        sems.at[len(copies)],
                    )
                )
            at += rows
            filled[out] += rows * size
    for copy in copies:
        copy.start()
    token_ref[...] = jnp.zeros(token_ref.shape, F32)
    for copy in copies:
        copy.wait()


def place_rows(pieces, size, table, first, targets, shapes, filled=(), behind=()):
    steps = len(pieces)
    copies = steps * sum(len(runs) for runs in targets)
    operands = [piece for step in pieces for piece in step]
    anywhere = pl.BlockSpec(memory_space=pl.ANY)
    *outs, token = pl.pallas_call(
        functools.partial(place_kernel, steps, size, first, targets, len(shapes), len(filled), len(behind)),
        out_shape=[jax.ShapeDtypeStruct(shape, F32) for shape in (*shapes, (8, 128))],
        in_specs=[IN_SMEM] + [IN_VMEM] * (len(behind) + len(operands)) + [anywhere] * len(filled),
        out_specs=[anywhere] * len(shapes) + [IN_VMEM],
        scratch_shapes=[pltpu.SemaphoreType.DMA((copies,))],
        input_output_aliases={1 + len(behind) + len(operands) + at: at for at in range(len(filled))},
        compiler_params=pltpu.CompilerParams(vmem_limit_bytes=SMALL_LIMIT),
        cost_estimate=QUICK,
    )(table, *behind, *operands, *filled)
    return outs, token


def add_kernel(step, spots_ref, *refs):
    count = len(refs) // 3
    for at in range(count):
        moved_ref, part_ref, out_ref = refs[at], refs[count + at], refs[2 * count + at]
        rows = moved_ref.shape[0]
        start = pl.multiple_of(spots_ref[step, at] * rows, 8)
        out_ref[...] = moved_ref[...] + part_ref[pl.ds(start, rows), :]


def add_pieces(moving, parts, table, step):
    return call(
        functools.partial(add_kernel, step),
        tuple(jax.ShapeDtypeStruct(held.shape, F32) for held in moving),
        (table, *moving, *parts),
        limit=SMALL_LIMIT,
    )


def ring_table(ways, size):
    order, place = ring_place(size)
    steps = jnp.arange(2 * size - 1, dtype=jnp.int32)[:, None]
    return (place - jnp.asarray(ways, jnp.int32)[None, :] * steps) % size


class Ring:
    def __init__(self, parts, firsts, ways, size, table):
        order, place = ring_place(size)
        self.perms = [[(order[at], order[(at + way) % size]) for at in range(size)] for way in ways]
        self.table = table
        self.parts, self.size, self.count = parts, size, 0
        self.moving = list(firsts)
        self.pieces = []

    def step(self, gate=None):
        if self.count == 2 * self.size - 2:
            return self.moving[0]
        self.count += 1
        self.moving = [lax.ppermute(held, "dp", perm) for held, perm in zip(self.moving, self.perms)]
        if gate is not None:
            self.moving = after(self.moving, gate)
        if self.count < self.size:
            self.moving = add_pieces(self.moving, self.parts, self.table, self.count)
        if self.count >= self.size - 1:
            self.pieces.append(self.moving)
        return self.moving[0]

    def finish(self, targets, shapes, gate=None):
        steps = 2 * self.size - 2
        if gate is None:
            while self.count < steps:
                self.step()
            return place_rows(self.pieces, self.size, self.table, self.size - 1, targets, shapes)
        while self.count < steps - 2:
            self.step()
        early = len(self.pieces)
        outs, token = place_rows(
            self.pieces, self.size, self.table, self.size - 1, targets, shapes, (), (gate,)
        )
        while self.count < steps:
            self.step()
        return place_rows(
            self.pieces[early:], self.size, self.table, self.size - 1 + early, targets, shapes, outs
        )


class Plain:
    def __init__(self, parts):
        self.parts = parts

    def step(self, gate=None):
        return self.parts[0]

    def finish(self, targets, shapes, gate=None):
        outs = [[] for shape in shapes]
        for part, runs in zip(lax.psum(self.parts, "dp"), targets):
            at = 0
            for share, out in runs:
                rows = part.shape[0] * share[0] // share[1]
                outs[out].append(part[at : at + rows])
                at += rows
        return [jnp.concatenate(rows, axis=0) for rows in outs], None


def whole_blocks(heights, size):
    return size <= 16 and size % 2 == 0 and all(height % (8 * size) == 0 for height in heights)


def start_sum(parts, firsts, ways, size, table, rings):
    return Ring(parts, firsts, ways, size, table) if rings else Plain(parts)


def column_sums(values):
    return jnp.sum(values.astype(F32), axis=0, keepdims=True)


def over_tokens(left, right):
    return lax.dot_general(left, right, (((0,), (0,)), ((), ())), preferred_element_type=F32)


def copy_block(spots_ref, at, part_ref, first_ref):
    rows = first_ref.shape[0]
    first_ref[...] = part_ref[pl.ds(pl.multiple_of(spots_ref[0, at] * rows, 8), rows), :]


def mlp_grads_kernel(
    spots_ref,
    flags_ref,
    mlp_in_ref,
    d_pre_ref,
    activated_ref,
    d_mlp_ref,
    down_weight_ref,
    up_ref,
    down_ref,
    bias_ref,
    up_first_ref,
    down_first_ref,
    mine_ref,
    theirs_ref,
    part_ref,
):
    up_ref[...] = over_tokens(mlp_in_ref[...], d_pre_ref[...])
    down_ref[...] = over_tokens(activated_ref[...], d_mlp_ref[...])
    bias_ref[0:1, :] = column_sums(d_pre_ref[...])
    bias_ref[1:2, :] = column_sums(d_mlp_ref[...])
    copy_block(spots_ref, 0, up_ref, up_first_ref)
    copy_block(spots_ref, 1, down_ref, down_first_ref)
    part_ref[...] = jnp.dot(activated_ref[...], down_weight_ref[...], preferred_element_type=F32)
    split_rows(flags_ref[0], part_ref, mine_ref, theirs_ref)


def attention_grads_kernel(
    blocks,
    spots_ref,
    heads_in_ref,
    d_queries_ref,
    d_keys_ref,
    d_values_ref,
    attended_ref,
    d_attn_ref,
    upper_ref,
    lower_ref,
    upper_first_ref,
    lower_first_ref,
    bias_ref,
):
    feats = d_queries_ref.shape[1]
    heads_in = heads_in_ref[...]
    upper_ref[0:feats, :] = over_tokens(d_queries_ref[...], heads_in)
    upper_ref[feats : 2 * feats, :] = over_tokens(d_keys_ref[...], heads_in)
    values_part = over_tokens(d_values_ref[...], heads_in)
    mixing_part = over_tokens(attended_ref[...].astype(BF16), d_attn_ref[...])
    run = feats // blocks
    for at in range(blocks):
        base = at * 2 * run
        lower_ref[base : base + run, :] = values_part[at * run : (at + 1) * run]
        lower_ref[base + run : base + 2 * run, :] = mixing_part[at * run : (at + 1) * run]
    bias_ref[...] = jnp.zeros(bias_ref.shape, F32)
    bias_ref[0:1, :] = column_sums(d_attn_ref[...])
    bias_ref[1:2, 0:feats] = column_sums(d_queries_ref[...])
    bias_ref[2:3, 0:feats] = column_sums(d_values_ref[...])
    copy_block(spots_ref, 0, upper_ref, upper_first_ref)
    copy_block(spots_ref, 1, lower_ref, lower_first_ref)


def of_rows(values):
    centered = values - jnp.mean(values, axis=-1, keepdims=True)
    inverse = lax.rsqrt(jnp.mean(centered * centered, axis=-1, keepdims=True) + 1e-06)
    return centered * inverse, inverse


def against_rows(left, right):
    return lax.dot_general(left, right, (((1,), (1,)), ((), ())), preferred_element_type=F32)


def times(left, right):
    return jnp.dot(left, right, preferred_element_type=F32)


def latent_rows(ref):
    return [slice(at * SEQ, (at + 1) * SEQ) for at in range(ref.shape[0] // SEQ)]


def head_columns(columns):
    return [slice(at * HEAD_DIM, (at + 1) * HEAD_DIM) for at in range(columns // HEAD_DIM)]


def softmax_rows(queries, key_rows):
    scores = against_rows(queries, key_rows) * HEAD_DIM ** (-0.5)
    exp_terms = jnp.exp(scores - jnp.max(scores, axis=-1, keepdims=True))
    return exp_terms / jnp.sum(exp_terms, axis=-1, keepdims=True)


def attend_kernel(
    table_ref, flags_ref, mixing_bias_ref, up_bias_ref, down_bias_ref, hidden_ref, scale_ref, shift_ref, weight_ref, bias_ref, heads_in_ref, queries_ref, keys_ref, values_ref, attended_ref
):
    feats = queries_ref.shape[1]
    bias = bias_ref[...].astype(F32)
    for at, rows in enumerate(latent_rows(hidden_ref)):
        normed, inverse = of_rows(hidden_ref[rows, :].astype(F32))
        heads_in = (normed * (1.0 + scale_ref[at : at + 1, :]) + shift_ref[at : at + 1, :]).astype(BF16)
        heads_in_ref[rows, :] = heads_in
        queries = (against_rows(heads_in, weight_ref[0:feats, :]) + bias[0:1]).astype(BF16)
        keys = against_rows(heads_in, weight_ref[feats : 2 * feats, :]).astype(BF16)
        values = (against_rows(heads_in, weight_ref[2 * feats : 3 * feats, :]) + bias[1:2]).astype(BF16)
        queries_ref[rows, :] = queries
        keys_ref[rows, :] = keys
        values_ref[rows, :] = values
        mixed = []
        for cols in head_columns(feats):
            weights = softmax_rows(queries[:, cols], keys[:, cols])
            mixed.append(times(weights.astype(BF16), values[:, cols]))
        attended_ref[rows, :] = jnp.concatenate(mixed, axis=1).astype(BF16).astype(F32)


def in_order(flags_ref, blocks):
    low, high = flags_ref[0] == 1, flags_ref[1] == 1
    return [
        jnp.where(
            high,
            jnp.where(low, blocks[at ^ 3], blocks[at ^ 2]),
            jnp.where(low, blocks[at ^ 1], blocks[at]),
        )
        for at in range(4)
    ]


def widen_kernel(first, values_ref, behind_ref, out_ref):
    out_ref[...] = values_ref[first : first + out_ref.shape[0], :].astype(F32)


def cotangent_kernel(cotangent_ref, gate_ref, down_ref, d_mlp_ref, d_act_ref):
    for at, rows in enumerate(latent_rows(cotangent_ref)):
        d_mlp = (cotangent_ref[rows, :].astype(F32) * gate_ref[at : at + 1, :]).astype(BF16)
        d_mlp_ref[rows, :] = d_mlp
        d_act_ref[rows, :] = against_rows(d_mlp, down_ref[...])


def mlp_kernel(
    odd_ref,
    own_ref,
    beside_ref,
    across_ref,
    corner_ref,
    mixing_0_ref,
    mixing_1_ref,
    mixing_2_ref,
    mixing_3_ref,
    mixing_4_ref,
    mixing_5_ref,
    mixing_6_ref,
    mixing_7_ref,
    mixing_bias_ref,
    hidden_ref,
    gate_ref,
    scale_ref,
    shift_ref,
    up_ref,
    up_bias_ref,
    d_act_ref,
    attn_out_ref,
    mlp_in_ref,
    activated_ref,
    d_pre_ref,
    mine_ref,
    theirs_ref,
    part_ref,
):
    odd = odd_ref[0]
    blocks = (own_ref, beside_ref, across_ref, corner_ref)
    mixing = in_order(
        odd_ref,
        [
            jnp.concatenate([top[...].astype(BF16), low[...].astype(BF16)], axis=0)
            for top, low in (
                (mixing_0_ref, mixing_1_ref),
                (mixing_2_ref, mixing_3_ref),
                (mixing_4_ref, mixing_5_ref),
                (mixing_6_ref, mixing_7_ref),
            )
        ],
    )
    for at, rows in enumerate(latent_rows(hidden_ref)):
        attn_out = mixing_bias_ref[...].astype(F32)
        for block, piece in enumerate(in_order(odd_ref, [ref[rows, :] for ref in blocks])):
            attn_out = attn_out + times(piece.astype(BF16), mixing[block])
        attn_out_ref[rows, :] = attn_out
        middle = hidden_ref[rows, :].astype(F32) + gate_ref[at : at + 1, :] * attn_out
        normed, inverse = of_rows(middle)
        mlp_in = (normed * (1.0 + scale_ref[at : at + 1, :]) + shift_ref[at : at + 1, :]).astype(BF16)
        mlp_in_ref[rows, :] = mlp_in
        pre_act = times(mlp_in, up_ref[...]) + up_bias_ref[...].astype(F32)
        square = pre_act * pre_act
        bend = jnp.tanh(GELU_SCALE * pre_act * (1.0 + 0.044715 * square))
        activated_ref[rows, :] = (0.5 * pre_act * (1.0 + bend)).astype(BF16)
        slope = 0.5 * (1.0 + bend) + 0.5 * pre_act * (1.0 - bend * bend) * (
            GELU_SCALE * (1.0 + 3.0 * 0.044715 * square)
        )
        d_pre = (d_act_ref[rows, :] * slope).astype(BF16)
        d_pre_ref[rows, :] = d_pre
        part_ref[rows, :] = against_rows(d_pre, up_ref[...])
    split_rows(odd, part_ref, mine_ref, theirs_ref)


def split_rows(odd, part_ref, mine_ref, theirs_ref):
    half = mine_ref.shape[0]
    mine_ref[...] = part_ref[pl.ds(pl.multiple_of(odd * half, 8), half), :]
    theirs_ref[...] = part_ref[pl.ds(pl.multiple_of((1 - odd) * half, 8), half), :]


def join_halves(odd, full_ref, other_ref, joined_ref):
    half = full_ref.shape[0]
    joined_ref[pl.ds(pl.multiple_of(odd * half, 8), half), :] = full_ref[...]
    joined_ref[pl.ds(pl.multiple_of((1 - odd) * half, 8), half), :] = other_ref[...]


def norm_grad(upstream, normed, inverse):
    mean_grad = jnp.mean(upstream, axis=-1, keepdims=True)
    mean_proj = jnp.mean(upstream * normed, axis=-1, keepdims=True)
    return inverse * (upstream - mean_grad - normed * mean_proj)


def middle_back_kernel(
    odd_ref,
    full_ref,
    other_ref,
    attn_out_ref,
    hidden_ref,
    cotangent_ref,
    gate_ref,
    scale_ref,
    d_middle_ref,
    d_attn_ref,
    d_shift_ref,
    d_scale_ref,
    d_gate_ref,
    joined_ref,
):
    join_halves(odd_ref[0], full_ref, other_ref, joined_ref)
    for at, rows in enumerate(latent_rows(hidden_ref)):
        gate = gate_ref[at : at + 1, :]
        attn_out = attn_out_ref[rows, :]
        normed, inverse = of_rows(hidden_ref[rows, :].astype(F32) + gate * attn_out)
        d_mlp_in = joined_ref[rows, :]
        d_shift_ref[at : at + 1, :] = jnp.sum(d_mlp_in, axis=0, keepdims=True)
        d_scale_ref[at : at + 1, :] = jnp.sum(d_mlp_in * normed, axis=0, keepdims=True)
        d_middle = cotangent_ref[rows, :].astype(F32) + norm_grad(
            d_mlp_in * (1.0 + scale_ref[at : at + 1, :]), normed, inverse
        )
        d_middle_ref[rows, :] = d_middle
        d_gate_ref[at : at + 1, :] = jnp.sum(d_middle * attn_out, axis=0, keepdims=True)
        d_attn_ref[rows, :] = (d_middle * gate).astype(BF16)


def attention_back_kernel(
    odd_ref,
    d_attn_ref,
    mixing_ref,
    queries_ref,
    keys_ref,
    values_ref,
    weight_ref,
    d_queries_ref,
    d_keys_ref,
    d_values_ref,
    mine_ref,
    theirs_ref,
    part_ref,
):
    feats = queries_ref.shape[1]
    scale = HEAD_DIM ** (-0.5)
    for rows in latent_rows(d_attn_ref):
        d_attended = against_rows(d_attn_ref[rows, :], mixing_ref[...]).astype(BF16)
        queries, keys, values = queries_ref[rows, :], keys_ref[rows, :], values_ref[rows, :]
        d_queries, d_keys, d_values = [], [], []
        for cols in head_columns(feats):
            weights = softmax_rows(queries[:, cols], keys[:, cols])
            d_weights = against_rows(d_attended[:, cols], values[:, cols])
            row_dots = jnp.sum(weights * d_weights, axis=-1, keepdims=True)
            d_scores = (weights * (d_weights - row_dots)).astype(BF16)
            d_queries.append(times(d_scores, keys[:, cols]) * scale)
            d_keys.append(over_tokens(d_scores, queries[:, cols]) * scale)
            d_values.append(over_tokens(weights.astype(BF16), d_attended[:, cols]))
        total = None
        for at, (ref, columns) in enumerate(
            ((d_queries_ref, d_queries), (d_keys_ref, d_keys), (d_values_ref, d_values))
        ):
            joined = jnp.concatenate(columns, axis=1).astype(BF16)
            ref[rows, :] = joined
            term = times(joined, weight_ref[at * feats : (at + 1) * feats, :])
            total = term if total is None else total + term
        part_ref[rows, :] = total
    split_rows(odd_ref[0], part_ref, mine_ref, theirs_ref)


def input_back_kernel(
    odd_ref, full_ref, other_ref, hidden_ref, d_middle_ref, scale_ref, input_grad_ref, d_shift_ref, d_scale_ref, joined_ref
):
    join_halves(odd_ref[0], full_ref, other_ref, joined_ref)
    for at, rows in enumerate(latent_rows(hidden_ref)):
        normed, inverse = of_rows(hidden_ref[rows, :].astype(F32))
        d_heads_in = joined_ref[rows, :]
        d_shift_ref[at : at + 1, :] = jnp.sum(d_heads_in, axis=0, keepdims=True)
        d_scale_ref[at : at + 1, :] = jnp.sum(d_heads_in * normed, axis=0, keepdims=True)
        input_grad_ref[rows, :] = d_middle_ref[rows, :] + norm_grad(
            d_heads_in * (1.0 + scale_ref[at : at + 1, :]), normed, inverse
        )


def block_out_kernel(
    odd_ref,
    full_ref,
    other_ref,
    bias_ref,
    attn_out_ref,
    hidden_ref,
    cotangent_ref,
    gate_one_ref,
    gate_two_ref,
    block_out_ref,
    d_gate_ref,
    joined_ref,
):
    join_halves(odd_ref[0], full_ref, other_ref, joined_ref)
    for at, rows in enumerate(latent_rows(hidden_ref)):
        mlp_out = joined_ref[rows, :] + bias_ref[...].astype(F32)
        middle = hidden_ref[rows, :].astype(F32) + gate_one_ref[at : at + 1, :] * attn_out_ref[rows, :]
        block_out_ref[rows, :] = (middle + gate_two_ref[at : at + 1, :] * mlp_out).astype(BF16)
        d_gate_ref[at : at + 1, :] = jnp.sum(
            cotangent_ref[rows, :].astype(F32) * mlp_out, axis=0, keepdims=True
        )


def sum_kernel(left_ref, right_ref, out_ref):
    out_ref[...] = left_ref[...] + right_ref[...]


def pack_kernel(
    flags_ref, shift_one, scale_one, gate_one, shift_two, scale_two, gate_two, mlp_bias_ref, heads_bias_ref, out_ref, all_ref
):
    latents, width = shift_one.shape
    columns = out_ref.shape[1]
    for at, ref in enumerate((shift_one, scale_one, gate_one, shift_two, scale_two, gate_two)):
        all_ref[:, at * width : (at + 1) * width] = ref[...]
    start = pl.multiple_of((flags_ref[0] + 2 * flags_ref[1]) * columns, 128)
    out_ref[...] = jnp.zeros(out_ref.shape, F32)
    out_ref[0:latents, :] = all_ref[:, pl.ds(start, columns)]
    out_ref[latents : latents + 2, 0:width] = mlp_bias_ref[...]
    out_ref[latents + 2 : latents + 5, 0:width] = heads_bias_ref[...]


def modulation_grad_kernel(
    latents, carried_ref, silu_ref, weight_ref, weight_grad_ref, bias_grad_ref, silu_grad_ref, bias_sum_ref
):
    groups = silu_ref.shape[0] // latents
    height = carried_ref.shape[0] // groups
    mods = jnp.concatenate(
        [carried_ref[at * height : at * height + latents, :] for at in range(groups)], axis=0
    ).astype(BF16)
    total = carried_ref[latents : latents + 5, :]
    for at in range(1, groups):
        total = total + carried_ref[at * height + latents : at * height + latents + 5, :]
    bias_sum_ref[...] = total
    weight_grad_ref[...] = lax.dot_general(
        silu_ref[...], mods, (((0,), (0,)), ((), ())), preferred_element_type=F32
    )
    bias_grad_ref[...] = jnp.sum(mods.astype(F32), axis=0, keepdims=True)
    silu_grad_ref[...] = lax.dot_general(
        mods, weight_ref[...], (((1,), (1,)), ((), ())), preferred_element_type=F32
    )


def after(values, gate):
    flat, tree = jax.tree.flatten(values)
    return jax.tree.unflatten(tree, lax.optimization_barrier((*flat, gate))[:-1])


def on_device(
    tensor_size,
    dp_size,
    hidden_in,
    out_cotangent,
    class_label,
    time_step,
    modulation_weight,
    modulation_bias,
    heads_weight,
    heads_bias,
    mixing_weight,
    mixing_bias,
    up_weight,
    up_bias,
    down_weight,
    down_bias,
    class_table,
    time_table,
):
    model_width = hidden_in.shape[1]
    own_latents = hidden_in.shape[0] // SEQ
    tok_rows = own_latents * SEQ
    lat_first = lax.axis_index("dp") * own_latents

    class_pick = jax.nn.one_hot(class_label, class_table.shape[0], dtype=BF16)
    time_pick = jax.nn.one_hot(time_step, time_table.shape[0], dtype=BF16)
    cond_part = jnp.dot(class_pick, class_table, preferred_element_type=F32) + jnp.dot(
        time_pick, time_table, preferred_element_type=F32
    )
    condition = join_columns(cond_part, tensor_size)
    silu_all = jax.nn.silu(condition).astype(BF16)
    silu_own = lax.dynamic_slice_in_dim(silu_all, lat_first, own_latents)
    mod_part = jnp.dot(silu_own, modulation_weight, preferred_element_type=F32) + modulation_bias.astype(F32)
    modulation = join_columns(mod_part, tensor_size)
    shift_one, scale_one, gate_one, shift_two, scale_two, gate_two = (
        modulation[:, number * model_width : (number + 1) * model_width] for number in range(6)
    )

    own_feats = heads_weight.shape[2]
    half = tok_rows // 2
    index = lax.axis_index("tensor")
    ways = (1, -1)
    table = ring_table(ways, dp_size)
    rings = whole_blocks((model_width, own_feats, up_weight.shape[1]), dp_size)
    flags = jnp.stack([index % 2, index // 2]).astype(jnp.int32)
    tokens = lambda dtype: jax.ShapeDtypeStruct((tok_rows, model_width), dtype)
    features = lambda dtype: jax.ShapeDtypeStruct((tok_rows, own_feats), dtype)
    halves = jax.ShapeDtypeStruct((half, model_width), F32)
    per_latent = jax.ShapeDtypeStruct((own_latents, model_width), F32)
    add = lambda left, right: call(sum_kernel, halves, (left, right), scalars=0, limit=SMALL_LIMIT)

    mixing_half = own_feats // 2
    mixing_own = [
        call(
            functools.partial(widen_kernel, first),
            jax.ShapeDtypeStruct((mixing_half, model_width), F32),
            (mixing_weight, behind),
            scalars=0,
            limit=SMALL_LIMIT,
        )
        for first, behind in ((0, cond_part), (mixing_half, gate_two))
    ]
    bias_rows = [bias.reshape(1, bias.shape[0]) for bias in (mixing_bias, up_bias, down_bias)]
    heads_rows = heads_weight.transpose(1, 2, 0).reshape(3 * own_feats, model_width)
    heads_in, queries, key_rows, value_rows, attended = call(
        attend_kernel,
        (tokens(BF16), features(BF16), features(BF16), features(BF16), features(F32)),
        (table, flags, *bias_rows, hidden_in, scale_one, shift_one, heads_rows, heads_bias),
        scalars=2,
    )
    mixing_far = [swap(rows, tensor_size, 2) for rows in mixing_own]
    attended_across = swap(attended, tensor_size, 2)
    attended_beside = swap(attended, tensor_size, 1)
    d_mlp, d_act = call(
        cotangent_kernel,
        (tokens(BF16), jax.ShapeDtypeStruct((tok_rows, down_weight.shape[0]), F32)),
        (after(out_cotangent, attended), gate_two, down_weight),
        scalars=0,
    )
    attended_across = after(attended_across, d_act)
    mixing_across = after(mixing_far, attended_across)
    mixing_blocks = (
        *mixing_own,
        *(swap(rows, tensor_size, 1) for rows in mixing_own),
        *mixing_across,
        *(swap(rows, tensor_size, 1) for rows in mixing_across),
    )
    attn_out, mlp_in, activated, d_pre, mine, theirs = call(
        mlp_kernel,
        (
            tokens(F32),
            tokens(BF16),
            jax.ShapeDtypeStruct((tok_rows, up_weight.shape[1]), BF16),
            jax.ShapeDtypeStruct((tok_rows, up_weight.shape[1]), BF16),
            halves,
            halves,
        ),
        (
            flags,
            attended,
            attended_beside,
            attended_across,
            swap(attended_across, tensor_size, 1),
            *mixing_blocks,
            bias_rows[0],
            hidden_in,
            gate_one,
            scale_two,
            shift_two,
            up_weight,
            bias_rows[1],
            d_act,
        ),
        scratch=[pltpu.VMEM((tok_rows, model_width), F32)],
    )
    chip_two = add(mine, swap(theirs, tensor_size, 1))

    activated, d_pre = after((activated, d_pre), chip_two)
    up_part, down_part, mlp_bias, up_first, down_first, mine, theirs = call(
        mlp_grads_kernel,
        (
            jax.ShapeDtypeStruct((model_width, d_pre.shape[1]), F32),
            jax.ShapeDtypeStruct((activated.shape[1], model_width), F32),
            jax.ShapeDtypeStruct((2, model_width), F32),
            jax.ShapeDtypeStruct((model_width // dp_size, d_pre.shape[1]), F32),
            jax.ShapeDtypeStruct((activated.shape[1] // dp_size, model_width), F32),
            halves,
            halves,
        ),
        (table, flags, mlp_in, d_pre, activated, d_mlp, down_weight),
        scalars=2,
        scratch=[pltpu.VMEM((tok_rows, model_width), F32)],
    )
    mlp_ring = start_sum((up_part, down_part), (up_first, down_first), ways, dp_size, table, rings)
    chip_out = add(mine, swap(theirs, tensor_size, 1))
    mlp_ring.step()
    across_two = after(after(swap(chip_two, tensor_size, 2), chip_out), mlp_ring.step())
    full_two = add(chip_two, across_two)
    chip_out = after(chip_out, full_two)
    out_across = swap(chip_out, tensor_size, 2)
    d_middle, d_attn, d_shift_two, d_scale_two, d_gate_one = call(
        middle_back_kernel,
        (tokens(F32), tokens(BF16), per_latent, per_latent, per_latent),
        (
            flags,
            full_two,
            swap(full_two, tensor_size, 1),
            attn_out,
            hidden_in,
            out_cotangent,
            gate_one,
            scale_two,
        ),
        scratch=[pltpu.VMEM((tok_rows, model_width), F32)],
    )
    d_attn = after(d_attn, mlp_ring.step(d_attn))
    d_queries, d_keys, d_values, mine, theirs = call(
        attention_back_kernel,
        (features(BF16), features(BF16), features(BF16), halves, halves),
        (flags, d_attn, mixing_weight, queries, key_rows, value_rows, heads_rows),
        scratch=[pltpu.VMEM((tok_rows, model_width), F32)],
    )
    beside_one = after(swap(theirs, tensor_size, 1), mlp_ring.step(theirs))
    full_out = add(chip_out, out_across)
    chip_one = after(add(mine, beside_one), full_out)
    out_other = swap(full_out, tensor_size, 1)

    d_queries, d_keys, d_values = after((d_queries, d_keys, d_values), chip_one)
    blocks = dp_size if rings else 1
    upper_rows, lower_rows = 2 * own_feats, 2 * own_feats
    upper_part, lower_part, upper_first, lower_first, heads_bias_part = call(
        functools.partial(attention_grads_kernel, blocks),
        (
            jax.ShapeDtypeStruct((upper_rows, model_width), F32),
            jax.ShapeDtypeStruct((lower_rows, model_width), F32),
            jax.ShapeDtypeStruct((upper_rows // dp_size, model_width), F32),
            jax.ShapeDtypeStruct((lower_rows // dp_size, model_width), F32),
            jax.ShapeDtypeStruct((3, model_width), F32),
        ),
        (table, heads_in, d_queries, d_keys, d_values, attended, d_attn),
    )
    heads_ring = start_sum((upper_part, lower_part), (upper_first, lower_first), ways, dp_size, table, rings)
    block_out, d_gate_two = call(
        block_out_kernel,
        (jax.ShapeDtypeStruct((tok_rows, model_width), BF16), per_latent),
        (
            flags,
            full_out,
            after(out_other, upper_first),
            bias_rows[2],
            attn_out,
            hidden_in,
            out_cotangent,
            gate_one,
            gate_two,
        ),
        scratch=[pltpu.VMEM((tok_rows, model_width), F32)],
    )
    gate = mlp_ring.step(heads_ring.step(d_gate_two))
    across_one = after(swap(chip_one, tensor_size, 2), gate)
    full_one = add(chip_one, across_one)
    input_grad, d_shift_one, d_scale_one = call(
        input_back_kernel,
        (jax.ShapeDtypeStruct((tok_rows, model_width), F32), per_latent, per_latent),
        (
            flags,
            full_one,
            swap(full_one, tensor_size, 1),
            hidden_in,
            d_middle,
            scale_one,
        ),
        scratch=[pltpu.VMEM((tok_rows, model_width), F32)],
    )
    own_cols = modulation_weight.shape[1]
    carried = -(-(own_latents + 5) // 8) * 8
    own_mods = call(
        pack_kernel,
        jax.ShapeDtypeStruct((carried, own_cols), F32),
        (
            flags,
            d_shift_one,
            d_scale_one,
            d_gate_one,
            d_shift_two,
            d_scale_two,
            d_gate_two,
            mlp_bias,
            heads_bias_part,
        ),
        scratch=[pltpu.VMEM((own_latents, 6 * model_width), F32)],
        limit=SMALL_LIMIT,
    )
    mlp_ring.step(own_mods)
    heads_ring.step(own_mods)
    whole = (1, 1)
    run = (1, 2)
    (heads_sum, mixing_weight_sum), placed = heads_ring.finish(
        (((whole, 0),), ((run, 0), (run, 1))),
        ((3 * own_feats, model_width), (own_feats, model_width)),
    )
    (up_weight_sum, down_weight_sum), placed = mlp_ring.finish(
        (((whole, 0),), ((whole, 1),)), (up_part.shape, down_part.shape), placed
    )
    heads_weight_sum = heads_sum.reshape(3, own_feats, model_width).transpose(2, 0, 1)
    all_mods = gather_latents(own_mods, dp_size)
    mod_weight_sum, mod_bias_row, d_silu_part, bias_sum = call(
        functools.partial(modulation_grad_kernel, own_latents),
        (
            jax.ShapeDtypeStruct((model_width, own_cols), F32),
            jax.ShapeDtypeStruct((1, own_cols), F32),
            jax.ShapeDtypeStruct((silu_all.shape[0], model_width), F32),
            jax.ShapeDtypeStruct((5, own_cols), F32),
        ),
        (all_mods, silu_all, modulation_weight),
        scalars=0,
    )
    mod_bias_sum = mod_bias_row.reshape(own_cols)
    up_bias_sum, down_bias_sum, mixing_bias_sum = (bias_sum[row, :model_width] for row in range(3))
    heads_bias_sum = bias_sum[3:5, :own_feats]
    d_silu_own = scatter_features(d_silu_part, tensor_size)
    sigmoid_part = jax.nn.sigmoid(cond_part)
    d_condition = d_silu_own * sigmoid_part * (1.0 + cond_part * (1.0 - sigmoid_part))
    exact = dict(preferred_element_type=F32, precision=lax.Precision.HIGHEST)
    class_sum = jnp.einsum("lk,lf->kf", class_pick.astype(F32), d_condition, **exact)
    time_sum = jnp.einsum("lk,lf->kf", time_pick.astype(F32), d_condition, **exact)
    return (
        block_out,
        input_grad,
        mod_weight_sum,
        mod_bias_sum,
        heads_weight_sum,
        heads_bias_sum,
        mixing_weight_sum,
        mixing_bias_sum,
        up_weight_sum,
        up_bias_sum,
        down_weight_sum,
        down_bias_sum,
        class_sum,
        time_sum,
    )


def solution(mesh):
    in_specs = (
        P("dp", None),
        P("dp", None),
        P(),
        P(),
        P(None, "tensor"),
        P("tensor"),
        P(None, None, "tensor"),
        P(None, "tensor"),
        P("tensor", None),
        P(),
        P(None, "tensor"),
        P("tensor"),
        P("tensor", None),
        P(),
        P(None, "tensor"),
        P(None, "tensor"),
    )
    out_specs = (
        P("dp", None),
        P("dp", None),
        P(None, "tensor"),
        P("tensor"),
        P(None, None, "tensor"),
        P(None, "tensor"),
        P("tensor", None),
        P(),
        P(None, "tensor"),
        P("tensor"),
        P("tensor", None),
        P(),
        P(None, "tensor"),
        P(None, "tensor"),
    )

    def run(*args):
        return on_device(mesh.shape["tensor"], mesh.shape["dp"], *args)

    return jax.shard_map(run, mesh=mesh, in_specs=in_specs, out_specs=out_specs, check_vma=False)
```

```python
import functools
import math

import jax
import jax.numpy as jnp
from jax import lax
from jax.experimental import pallas as pl
from jax.experimental.pallas import tpu as pltpu
from jax.sharding import PartitionSpec as P

SEQ = 256
HEAD_DIM = 64
F32 = jnp.float32
BF16 = jnp.bfloat16


def swap(values, size, bit):
    return lax.ppermute(values, "tensor", [(at, at ^ bit) for at in range(size)])


def ring_place(size):
    order = list(range(0, size, 2)) + list(range(size - 1, 0, -2))
    index = lax.axis_index("dp")
    place = jnp.where(index % 2 == 0, index // 2, size - 1 - index // 2)
    return order, place


def gather_latents(own, size):
    if size % 2 or size > 16:
        return lax.all_gather(own, "dp", axis=0, tiled=True)
    rows = own.shape[0]
    index = lax.axis_index("dp")
    other = lax.ppermute(own, "dp", [(at, at ^ 1) for at in range(size)])
    odd = index % 2 == 1
    pair = jnp.concatenate([jnp.where(odd, other, own), jnp.where(odd, own, other)], axis=0)
    out = jnp.zeros((size * rows, own.shape[1]), own.dtype)
    out = lax.dynamic_update_slice_in_dim(out, pair, (index // 2) * 2 * rows, 0)
    for step in range(2, size, 2):
        got = lax.ppermute(pair, "dp", [(at, (at + step) % size) for at in range(size)])
        out = lax.dynamic_update_slice_in_dim(out, got, (((index - step) % size) // 2) * 2 * rows, 0)
    return out


def scatter_features(part, size):
    index = lax.axis_index("tensor")
    columns = part.shape[1] // size
    block = lambda at: lax.dynamic_slice_in_dim(part, at * columns, columns, 1)
    total = block(index)
    for bit in range(1, size):
        total = total + swap(block(index ^ bit), size, bit)
    return total


VMEM_LIMIT = 14 * 1024 * 1024
SMALL_LIMIT = 6 * 1024 * 1024
GELU_SCALE = (2.0 / math.pi) ** 0.5
IN_VMEM = pl.BlockSpec(memory_space=pltpu.VMEM)
IN_SMEM = pl.BlockSpec(memory_space=pltpu.SMEM)


QUICK = pl.CostEstimate(flops=1, transcendentals=0, bytes_accessed=1)


def call(kernel, out_shape, operands, scalars=1, scratch=(), limit=VMEM_LIMIT):
    single = not isinstance(out_shape, tuple)
    return pl.pallas_call(
        kernel,
        out_shape=out_shape,
        in_specs=[IN_SMEM] * scalars + [IN_VMEM] * (len(operands) - scalars),
        out_specs=IN_VMEM if single else [IN_VMEM] * len(out_shape),
        scratch_shapes=list(scratch),
        compiler_params=pltpu.CompilerParams(vmem_limit_bytes=limit),
        cost_estimate=QUICK,
    )(*operands)


def natural(blocks):
    index = lax.axis_index("tensor")
    low, high = index % 2 == 1, index >= 2
    return [
        jnp.where(
            high,
            jnp.where(low, blocks[at ^ 3], blocks[at ^ 2]),
            jnp.where(low, blocks[at ^ 1], blocks[at]),
        )
        for at in range(4)
    ]


def join_columns(own, size):
    blocks = [own] + [swap(own, size, bit) for bit in range(1, size)]
    return jnp.concatenate(natural(blocks), axis=1)


def place_kernel(steps, size, first, targets, outs, kept, spots_ref, *refs):
    count = len(targets)
    pieces = refs[: steps * count]
    out_refs = refs[steps * count + kept : steps * count + kept + outs]
    token_ref, sems = refs[-2], refs[-1]
    copies = []
    filled = [0] * outs
    for entry, runs in enumerate(targets):
        height = pieces[entry].shape[0]
        at = 0
        for share, out in runs:
            rows = height * share[0] // share[1]
            for step in range(steps):
                start = pl.multiple_of(spots_ref[first + step, entry] * rows + filled[out], 8)
                copies.append(
                    pltpu.make_async_copy(
                        pieces[step * count + entry].at[pl.ds(at, rows), :],
                        out_refs[out].at[pl.ds(start, rows), :],
                        sems.at[len(copies)],
                    )
                )
            at += rows
            filled[out] += rows * size
    for copy in copies:
        copy.start()
    token_ref[...] = jnp.zeros(token_ref.shape, F32)
    for copy in copies:
        copy.wait()


def place_rows(pieces, size, table, first, targets, shapes, filled=()):
    steps = len(pieces)
    copies = steps * sum(len(runs) for runs in targets)
    operands = [piece for step in pieces for piece in step]
    anywhere = pl.BlockSpec(memory_space=pl.ANY)
    *outs, token = pl.pallas_call(
        functools.partial(place_kernel, steps, size, first, targets, len(shapes), len(filled)),
        out_shape=[jax.ShapeDtypeStruct(shape, F32) for shape in (*shapes, (8, 128))],
        in_specs=[IN_SMEM] + [IN_VMEM] * len(operands) + [anywhere] * len(filled),
        out_specs=[anywhere] * len(shapes) + [IN_VMEM],
        scratch_shapes=[pltpu.SemaphoreType.DMA((copies,))],
        input_output_aliases={1 + len(operands) + at: at for at in range(len(filled))},
        compiler_params=pltpu.CompilerParams(vmem_limit_bytes=SMALL_LIMIT),
        cost_estimate=QUICK,
    )(table, *operands, *filled)
    return outs, token


def add_kernel(step, spots_ref, *refs):
    count = len(refs) // 3
    for at in range(count):
        moved_ref, part_ref, out_ref = refs[at], refs[count + at], refs[2 * count + at]
        rows = moved_ref.shape[0]
        start = pl.multiple_of(spots_ref[step, at] * rows, 8)
        out_ref[...] = moved_ref[...] + part_ref[pl.ds(start, rows), :]


def add_pieces(moving, parts, table, step):
    return call(
        functools.partial(add_kernel, step),
        tuple(jax.ShapeDtypeStruct(held.shape, F32) for held in moving),
        (table, *moving, *parts),
        limit=SMALL_LIMIT,
    )


def ring_table(ways, size):
    order, place = ring_place(size)
    steps = jnp.arange(2 * size - 1, dtype=jnp.int32)[:, None]
    return (place - jnp.asarray(ways, jnp.int32)[None, :] * steps) % size


class Ring:
    def __init__(self, parts, firsts, ways, size, table):
        order, place = ring_place(size)
        self.perms = [[(order[at], order[(at + way) % size]) for at in range(size)] for way in ways]
        self.table = table
        self.parts, self.size, self.count = parts, size, 0
        self.moving = list(firsts)
        self.pieces = []

    def step(self, gate=None):
        if self.count == 2 * self.size - 2:
            return self.moving[0]
        self.count += 1
        self.moving = [lax.ppermute(held, "dp", perm) for held, perm in zip(self.moving, self.perms)]
        if gate is not None:
            self.moving = after(self.moving, gate)
        if self.count < self.size:
            self.moving = add_pieces(self.moving, self.parts, self.table, self.count)
        if self.count >= self.size - 1:
            self.pieces.append(self.moving)
        return self.moving[0]

    def finish(self, targets, shapes, gate=None):
        steps = 2 * self.size - 2
        while self.count < steps - 2:
            self.step()
        early = len(self.pieces)
        outs, token = place_rows(self.pieces, self.size, self.table, self.size - 1, targets, shapes)
        self.step(token)
        if gate is not None:
            self.moving = after(self.moving, gate)
        self.step()
        return place_rows(
            self.pieces[early:], self.size, self.table, self.size - 1 + early, targets, shapes, outs
        )


class Plain:
    def __init__(self, parts):
        self.parts = parts

    def step(self, gate=None):
        return self.parts[0]

    def finish(self, targets, shapes, gate=None):
        outs = [[] for shape in shapes]
        for part, runs in zip(lax.psum(self.parts, "dp"), targets):
            at = 0
            for share, out in runs:
                rows = part.shape[0] * share[0] // share[1]
                outs[out].append(part[at : at + rows])
                at += rows
        return [jnp.concatenate(rows, axis=0) for rows in outs], None


def whole_blocks(heights, size):
    return size <= 16 and size % 2 == 0 and all(height % (8 * size) == 0 for height in heights)


def start_sum(parts, firsts, ways, size, table, rings):
    return Ring(parts, firsts, ways, size, table) if rings else Plain(parts)


def column_sums(values):
    return jnp.sum(values.astype(F32), axis=0, keepdims=True)


def over_tokens(left, right):
    return lax.dot_general(left, right, (((0,), (0,)), ((), ())), preferred_element_type=F32)


def copy_block(spots_ref, at, part_ref, first_ref):
    rows = first_ref.shape[0]
    first_ref[...] = part_ref[pl.ds(pl.multiple_of(spots_ref[0, at] * rows, 8), rows), :]


def mlp_grads_kernel(
    spots_ref,
    flags_ref,
    mlp_in_ref,
    d_pre_ref,
    activated_ref,
    d_mlp_ref,
    down_weight_ref,
    up_ref,
    down_ref,
    bias_ref,
    up_first_ref,
    down_first_ref,
    mine_ref,
    theirs_ref,
    part_ref,
):
    up_ref[...] = over_tokens(mlp_in_ref[...], d_pre_ref[...])
    down_ref[...] = over_tokens(activated_ref[...], d_mlp_ref[...])
    bias_ref[0:1, :] = column_sums(d_pre_ref[...])
    bias_ref[1:2, :] = column_sums(d_mlp_ref[...])
    copy_block(spots_ref, 0, up_ref, up_first_ref)
    copy_block(spots_ref, 1, down_ref, down_first_ref)
    part_ref[...] = jnp.dot(activated_ref[...], down_weight_ref[...], preferred_element_type=F32)
    split_rows(flags_ref[0], part_ref, mine_ref, theirs_ref)


def attention_grads_kernel(
    blocks,
    spots_ref,
    heads_in_ref,
    d_queries_ref,
    d_keys_ref,
    d_values_ref,
    attended_ref,
    d_attn_ref,
    upper_ref,
    lower_ref,
    upper_first_ref,
    lower_first_ref,
    bias_ref,
):
    feats = d_queries_ref.shape[1]
    heads_in = heads_in_ref[...]
    upper_ref[0:feats, :] = over_tokens(d_queries_ref[...], heads_in)
    upper_ref[feats : 2 * feats, :] = over_tokens(d_keys_ref[...], heads_in)
    values_part = over_tokens(d_values_ref[...], heads_in)
    mixing_part = over_tokens(attended_ref[...].astype(BF16), d_attn_ref[...])
    run = feats // blocks
    for at in range(blocks):
        base = at * 2 * run
        lower_ref[base : base + run, :] = values_part[at * run : (at + 1) * run]
        lower_ref[base + run : base + 2 * run, :] = mixing_part[at * run : (at + 1) * run]
    bias_ref[...] = jnp.zeros(bias_ref.shape, F32)
    bias_ref[0:1, :] = column_sums(d_attn_ref[...])
    bias_ref[1:2, 0:feats] = column_sums(d_queries_ref[...])
    bias_ref[2:3, 0:feats] = column_sums(d_values_ref[...])
    copy_block(spots_ref, 0, upper_ref, upper_first_ref)
    copy_block(spots_ref, 1, lower_ref, lower_first_ref)


def of_rows(values):
    centered = values - jnp.mean(values, axis=-1, keepdims=True)
    inverse = lax.rsqrt(jnp.mean(centered * centered, axis=-1, keepdims=True) + 1e-06)
    return centered * inverse, inverse


def against_rows(left, right):
    return lax.dot_general(left, right, (((1,), (1,)), ((), ())), preferred_element_type=F32)


def times(left, right):
    return jnp.dot(left, right, preferred_element_type=F32)


def latent_rows(ref):
    return [slice(at * SEQ, (at + 1) * SEQ) for at in range(ref.shape[0] // SEQ)]


def head_columns(columns):
    return [slice(at * HEAD_DIM, (at + 1) * HEAD_DIM) for at in range(columns // HEAD_DIM)]


def softmax_rows(queries, key_rows):
    scores = against_rows(queries, key_rows) * HEAD_DIM ** (-0.5)
    exp_terms = jnp.exp(scores - jnp.max(scores, axis=-1, keepdims=True))
    return exp_terms / jnp.sum(exp_terms, axis=-1, keepdims=True)


def attend_kernel(
    table_ref, flags_ref, mixing_bias_ref, up_bias_ref, down_bias_ref, hidden_ref, scale_ref, shift_ref, weight_ref, bias_ref, heads_in_ref, queries_ref, keys_ref, values_ref, attended_ref
):
    feats = queries_ref.shape[1]
    bias = bias_ref[...].astype(F32)
    for at, rows in enumerate(latent_rows(hidden_ref)):
        normed, inverse = of_rows(hidden_ref[rows, :].astype(F32))
        heads_in = (normed * (1.0 + scale_ref[at : at + 1, :]) + shift_ref[at : at + 1, :]).astype(BF16)
        heads_in_ref[rows, :] = heads_in
        queries = (against_rows(heads_in, weight_ref[0:feats, :]) + bias[0:1]).astype(BF16)
        keys = against_rows(heads_in, weight_ref[feats : 2 * feats, :]).astype(BF16)
        values = (against_rows(heads_in, weight_ref[2 * feats : 3 * feats, :]) + bias[1:2]).astype(BF16)
        queries_ref[rows, :] = queries
        keys_ref[rows, :] = keys
        values_ref[rows, :] = values
        mixed = []
        for cols in head_columns(feats):
            weights = softmax_rows(queries[:, cols], keys[:, cols])
            mixed.append(times(weights.astype(BF16), values[:, cols]))
        attended_ref[rows, :] = jnp.concatenate(mixed, axis=1).astype(BF16).astype(F32)


def in_order(flags_ref, blocks):
    low, high = flags_ref[0] == 1, flags_ref[1] == 1
    return [
        jnp.where(
            high,
            jnp.where(low, blocks[at ^ 3], blocks[at ^ 2]),
            jnp.where(low, blocks[at ^ 1], blocks[at]),
        )
        for at in range(4)
    ]


def widen_kernel(first, values_ref, behind_ref, out_ref):
    out_ref[...] = values_ref[first : first + out_ref.shape[0], :].astype(F32)


def cotangent_kernel(cotangent_ref, gate_ref, down_ref, d_mlp_ref, d_act_ref):
    for at, rows in enumerate(latent_rows(cotangent_ref)):
        d_mlp = (cotangent_ref[rows, :].astype(F32) * gate_ref[at : at + 1, :]).astype(BF16)
        d_mlp_ref[rows, :] = d_mlp
        d_act_ref[rows, :] = against_rows(d_mlp, down_ref[...])


def mlp_kernel(
    odd_ref,
    own_ref,
    beside_ref,
    across_ref,
    corner_ref,
    mixing_0_ref,
    mixing_1_ref,
    mixing_2_ref,
    mixing_3_ref,
    mixing_4_ref,
    mixing_5_ref,
    mixing_6_ref,
    mixing_7_ref,
    mixing_bias_ref,
    hidden_ref,
    gate_ref,
    scale_ref,
    shift_ref,
    up_ref,
    up_bias_ref,
    d_act_ref,
    attn_out_ref,
    mlp_in_ref,
    activated_ref,
    d_pre_ref,
    mine_ref,
    theirs_ref,
    part_ref,
):
    odd = odd_ref[0]
    blocks = (own_ref, beside_ref, across_ref, corner_ref)
    mixing = in_order(
        odd_ref,
        [
            jnp.concatenate([top[...].astype(BF16), low[...].astype(BF16)], axis=0)
            for top, low in (
                (mixing_0_ref, mixing_1_ref),
                (mixing_2_ref, mixing_3_ref),
                (mixing_4_ref, mixing_5_ref),
                (mixing_6_ref, mixing_7_ref),
            )
        ],
    )
    for at, rows in enumerate(latent_rows(hidden_ref)):
        attn_out = mixing_bias_ref[...].astype(F32)
        for block, piece in enumerate(in_order(odd_ref, [ref[rows, :] for ref in blocks])):
            attn_out = attn_out + times(piece.astype(BF16), mixing[block])
        attn_out_ref[rows, :] = attn_out
        middle = hidden_ref[rows, :].astype(F32) + gate_ref[at : at + 1, :] * attn_out
        normed, inverse = of_rows(middle)
        mlp_in = (normed * (1.0 + scale_ref[at : at + 1, :]) + shift_ref[at : at + 1, :]).astype(BF16)
        mlp_in_ref[rows, :] = mlp_in
        pre_act = times(mlp_in, up_ref[...]) + up_bias_ref[...].astype(F32)
        square = pre_act * pre_act
        bend = jnp.tanh(GELU_SCALE * pre_act * (1.0 + 0.044715 * square))
        activated_ref[rows, :] = (0.5 * pre_act * (1.0 + bend)).astype(BF16)
        slope = 0.5 * (1.0 + bend) + 0.5 * pre_act * (1.0 - bend * bend) * (
            GELU_SCALE * (1.0 + 3.0 * 0.044715 * square)
        )
        d_pre = (d_act_ref[rows, :] * slope).astype(BF16)
        d_pre_ref[rows, :] = d_pre
        part_ref[rows, :] = against_rows(d_pre, up_ref[...])
    split_rows(odd, part_ref, mine_ref, theirs_ref)


def split_rows(odd, part_ref, mine_ref, theirs_ref):
    half = mine_ref.shape[0]
    mine_ref[...] = part_ref[pl.ds(pl.multiple_of(odd * half, 8), half), :]
    theirs_ref[...] = part_ref[pl.ds(pl.multiple_of((1 - odd) * half, 8), half), :]


def join_halves(odd, full_ref, other_ref, joined_ref):
    half = full_ref.shape[0]
    joined_ref[pl.ds(pl.multiple_of(odd * half, 8), half), :] = full_ref[...]
    joined_ref[pl.ds(pl.multiple_of((1 - odd) * half, 8), half), :] = other_ref[...]


def norm_grad(upstream, normed, inverse):
    mean_grad = jnp.mean(upstream, axis=-1, keepdims=True)
    mean_proj = jnp.mean(upstream * normed, axis=-1, keepdims=True)
    return inverse * (upstream - mean_grad - normed * mean_proj)


def middle_back_kernel(
    odd_ref,
    full_ref,
    other_ref,
    attn_out_ref,
    hidden_ref,
    cotangent_ref,
    gate_ref,
    scale_ref,
    d_middle_ref,
    d_attn_ref,
    d_shift_ref,
    d_scale_ref,
    d_gate_ref,
    joined_ref,
):
    join_halves(odd_ref[0], full_ref, other_ref, joined_ref)
    for at, rows in enumerate(latent_rows(hidden_ref)):
        gate = gate_ref[at : at + 1, :]
        attn_out = attn_out_ref[rows, :]
        normed, inverse = of_rows(hidden_ref[rows, :].astype(F32) + gate * attn_out)
        d_mlp_in = joined_ref[rows, :]
        d_shift_ref[at : at + 1, :] = jnp.sum(d_mlp_in, axis=0, keepdims=True)
        d_scale_ref[at : at + 1, :] = jnp.sum(d_mlp_in * normed, axis=0, keepdims=True)
        d_middle = cotangent_ref[rows, :].astype(F32) + norm_grad(
            d_mlp_in * (1.0 + scale_ref[at : at + 1, :]), normed, inverse
        )
        d_middle_ref[rows, :] = d_middle
        d_gate_ref[at : at + 1, :] = jnp.sum(d_middle * attn_out, axis=0, keepdims=True)
        d_attn_ref[rows, :] = (d_middle * gate).astype(BF16)


def attention_back_kernel(
    odd_ref,
    d_attn_ref,
    mixing_ref,
    queries_ref,
    keys_ref,
    values_ref,
    weight_ref,
    d_queries_ref,
    d_keys_ref,
    d_values_ref,
    mine_ref,
    theirs_ref,
    part_ref,
):
    feats = queries_ref.shape[1]
    scale = HEAD_DIM ** (-0.5)
    for rows in latent_rows(d_attn_ref):
        d_attended = against_rows(d_attn_ref[rows, :], mixing_ref[...]).astype(BF16)
        queries, keys, values = queries_ref[rows, :], keys_ref[rows, :], values_ref[rows, :]
        d_queries, d_keys, d_values = [], [], []
        for cols in head_columns(feats):
            weights = softmax_rows(queries[:, cols], keys[:, cols])
            d_weights = against_rows(d_attended[:, cols], values[:, cols])
            row_dots = jnp.sum(weights * d_weights, axis=-1, keepdims=True)
            d_scores = (weights * (d_weights - row_dots)).astype(BF16)
            d_queries.append(times(d_scores, keys[:, cols]) * scale)
            d_keys.append(over_tokens(d_scores, queries[:, cols]) * scale)
            d_values.append(over_tokens(weights.astype(BF16), d_attended[:, cols]))
        total = None
        for at, (ref, columns) in enumerate(
            ((d_queries_ref, d_queries), (d_keys_ref, d_keys), (d_values_ref, d_values))
        ):
            joined = jnp.concatenate(columns, axis=1).astype(BF16)
            ref[rows, :] = joined
            term = times(joined, weight_ref[at * feats : (at + 1) * feats, :])
            total = term if total is None else total + term
        part_ref[rows, :] = total
    split_rows(odd_ref[0], part_ref, mine_ref, theirs_ref)


def input_back_kernel(
    odd_ref, full_ref, other_ref, hidden_ref, d_middle_ref, scale_ref, input_grad_ref, d_shift_ref, d_scale_ref, joined_ref
):
    join_halves(odd_ref[0], full_ref, other_ref, joined_ref)
    for at, rows in enumerate(latent_rows(hidden_ref)):
        normed, inverse = of_rows(hidden_ref[rows, :].astype(F32))
        d_heads_in = joined_ref[rows, :]
        d_shift_ref[at : at + 1, :] = jnp.sum(d_heads_in, axis=0, keepdims=True)
        d_scale_ref[at : at + 1, :] = jnp.sum(d_heads_in * normed, axis=0, keepdims=True)
        input_grad_ref[rows, :] = d_middle_ref[rows, :] + norm_grad(
            d_heads_in * (1.0 + scale_ref[at : at + 1, :]), normed, inverse
        )


def block_out_kernel(
    odd_ref,
    full_ref,
    other_ref,
    bias_ref,
    attn_out_ref,
    hidden_ref,
    cotangent_ref,
    gate_one_ref,
    gate_two_ref,
    block_out_ref,
    d_gate_ref,
    joined_ref,
):
    join_halves(odd_ref[0], full_ref, other_ref, joined_ref)
    for at, rows in enumerate(latent_rows(hidden_ref)):
        mlp_out = joined_ref[rows, :] + bias_ref[...].astype(F32)
        middle = hidden_ref[rows, :].astype(F32) + gate_one_ref[at : at + 1, :] * attn_out_ref[rows, :]
        block_out_ref[rows, :] = (middle + gate_two_ref[at : at + 1, :] * mlp_out).astype(BF16)
        d_gate_ref[at : at + 1, :] = jnp.sum(
            cotangent_ref[rows, :].astype(F32) * mlp_out, axis=0, keepdims=True
        )


def sum_kernel(left_ref, right_ref, out_ref):
    out_ref[...] = left_ref[...] + right_ref[...]


def pack_kernel(
    flags_ref, shift_one, scale_one, gate_one, shift_two, scale_two, gate_two, mlp_bias_ref, heads_bias_ref, out_ref, all_ref
):
    latents, width = shift_one.shape
    columns = out_ref.shape[1]
    for at, ref in enumerate((shift_one, scale_one, gate_one, shift_two, scale_two, gate_two)):
        all_ref[:, at * width : (at + 1) * width] = ref[...]
    start = pl.multiple_of((flags_ref[0] + 2 * flags_ref[1]) * columns, 128)
    out_ref[...] = jnp.zeros(out_ref.shape, F32)
    out_ref[0:latents, :] = all_ref[:, pl.ds(start, columns)]
    out_ref[latents : latents + 2, 0:width] = mlp_bias_ref[...]
    out_ref[latents + 2 : latents + 5, 0:width] = heads_bias_ref[...]


def modulation_grad_kernel(
    latents, carried_ref, silu_ref, weight_ref, weight_grad_ref, bias_grad_ref, silu_grad_ref, bias_sum_ref
):
    groups = silu_ref.shape[0] // latents
    height = carried_ref.shape[0] // groups
    mods = jnp.concatenate(
        [carried_ref[at * height : at * height + latents, :] for at in range(groups)], axis=0
    ).astype(BF16)
    total = carried_ref[latents : latents + 5, :]
    for at in range(1, groups):
        total = total + carried_ref[at * height + latents : at * height + latents + 5, :]
    bias_sum_ref[...] = total
    weight_grad_ref[...] = lax.dot_general(
        silu_ref[...], mods, (((0,), (0,)), ((), ())), preferred_element_type=F32
    )
    bias_grad_ref[...] = jnp.sum(mods.astype(F32), axis=0, keepdims=True)
    silu_grad_ref[...] = lax.dot_general(
        mods, weight_ref[...], (((1,), (1,)), ((), ())), preferred_element_type=F32
    )


def after(values, gate):
    flat, tree = jax.tree.flatten(values)
    return jax.tree.unflatten(tree, lax.optimization_barrier((*flat, gate))[:-1])


def on_device(
    tensor_size,
    dp_size,
    hidden_in,
    out_cotangent,
    class_label,
    time_step,
    modulation_weight,
    modulation_bias,
    heads_weight,
    heads_bias,
    mixing_weight,
    mixing_bias,
    up_weight,
    up_bias,
    down_weight,
    down_bias,
    class_table,
    time_table,
):
    model_width = hidden_in.shape[1]
    own_latents = hidden_in.shape[0] // SEQ
    tok_rows = own_latents * SEQ
    lat_first = lax.axis_index("dp") * own_latents

    class_pick = jax.nn.one_hot(class_label, class_table.shape[0], dtype=BF16)
    time_pick = jax.nn.one_hot(time_step, time_table.shape[0], dtype=BF16)
    cond_part = jnp.dot(class_pick, class_table, preferred_element_type=F32) + jnp.dot(
        time_pick, time_table, preferred_element_type=F32
    )
    condition = join_columns(cond_part, tensor_size)
    silu_all = jax.nn.silu(condition).astype(BF16)
    silu_own = lax.dynamic_slice_in_dim(silu_all, lat_first, own_latents)
    mod_part = jnp.dot(silu_own, modulation_weight, preferred_element_type=F32) + modulation_bias.astype(F32)
    modulation = join_columns(mod_part, tensor_size)
    shift_one, scale_one, gate_one, shift_two, scale_two, gate_two = (
        modulation[:, number * model_width : (number + 1) * model_width] for number in range(6)
    )

    own_feats = heads_weight.shape[2]
    half = tok_rows // 2
    index = lax.axis_index("tensor")
    ways = (1, -1)
    table = ring_table(ways, dp_size)
    rings = whole_blocks((model_width, own_feats, up_weight.shape[1]), dp_size)
    flags = jnp.stack([index % 2, index // 2]).astype(jnp.int32)
    tokens = lambda dtype: jax.ShapeDtypeStruct((tok_rows, model_width), dtype)
    features = lambda dtype: jax.ShapeDtypeStruct((tok_rows, own_feats), dtype)
    halves = jax.ShapeDtypeStruct((half, model_width), F32)
    per_latent = jax.ShapeDtypeStruct((own_latents, model_width), F32)
    add = lambda left, right: call(sum_kernel, halves, (left, right), scalars=0, limit=SMALL_LIMIT)

    mixing_half = own_feats // 2
    mixing_own = [
        call(
            functools.partial(widen_kernel, first),
            jax.ShapeDtypeStruct((mixing_half, model_width), F32),
            (mixing_weight, behind),
            scalars=0,
            limit=SMALL_LIMIT,
        )
        for first, behind in ((0, cond_part), (mixing_half, gate_two))
    ]
    bias_rows = [bias.reshape(1, bias.shape[0]) for bias in (mixing_bias, up_bias, down_bias)]
    heads_rows = heads_weight.transpose(1, 2, 0).reshape(3 * own_feats, model_width)
    heads_in, queries, key_rows, value_rows, attended = call(
        attend_kernel,
        (tokens(BF16), features(BF16), features(BF16), features(BF16), features(F32)),
        (table, flags, *bias_rows, hidden_in, scale_one, shift_one, heads_rows, heads_bias),
        scalars=2,
    )
    mixing_far = [swap(rows, tensor_size, 2) for rows in mixing_own]
    attended_across = swap(attended, tensor_size, 2)
    attended_beside = swap(attended, tensor_size, 1)
    d_mlp, d_act = call(
        cotangent_kernel,
        (tokens(BF16), jax.ShapeDtypeStruct((tok_rows, down_weight.shape[0]), F32)),
        (after(out_cotangent, attended), gate_two, down_weight),
        scalars=0,
    )
    attended_across = after(attended_across, d_act)
    mixing_across = after(mixing_far, attended_across)
    mixing_blocks = (
        *mixing_own,
        *(swap(rows, tensor_size, 1) for rows in mixing_own),
        *mixing_across,
        *(swap(rows, tensor_size, 1) for rows in mixing_across),
    )
    attn_out, mlp_in, activated, d_pre, mine, theirs = call(
        mlp_kernel,
        (
            tokens(F32),
            tokens(BF16),
            jax.ShapeDtypeStruct((tok_rows, up_weight.shape[1]), BF16),
            jax.ShapeDtypeStruct((tok_rows, up_weight.shape[1]), BF16),
            halves,
            halves,
        ),
        (
            flags,
            attended,
            attended_beside,
            attended_across,
            swap(attended_across, tensor_size, 1),
            *mixing_blocks,
            bias_rows[0],
            hidden_in,
            gate_one,
            scale_two,
            shift_two,
            up_weight,
            bias_rows[1],
            d_act,
        ),
        scratch=[pltpu.VMEM((tok_rows, model_width), F32)],
    )
    chip_two = add(mine, swap(theirs, tensor_size, 1))

    activated, d_pre = after((activated, d_pre), chip_two)
    up_part, down_part, mlp_bias, up_first, down_first, mine, theirs = call(
        mlp_grads_kernel,
        (
            jax.ShapeDtypeStruct((model_width, d_pre.shape[1]), F32),
            jax.ShapeDtypeStruct((activated.shape[1], model_width), F32),
            jax.ShapeDtypeStruct((2, model_width), F32),
            jax.ShapeDtypeStruct((model_width // dp_size, d_pre.shape[1]), F32),
            jax.ShapeDtypeStruct((activated.shape[1] // dp_size, model_width), F32),
            halves,
            halves,
        ),
        (table, flags, mlp_in, d_pre, activated, d_mlp, down_weight),
        scalars=2,
        scratch=[pltpu.VMEM((tok_rows, model_width), F32)],
    )
    mlp_ring = start_sum((up_part, down_part), (up_first, down_first), ways, dp_size, table, rings)
    chip_out = add(mine, swap(theirs, tensor_size, 1))
    mlp_ring.step()
    across_two = after(after(swap(chip_two, tensor_size, 2), chip_out), mlp_ring.step())
    full_two = add(chip_two, across_two)
    chip_out = after(chip_out, full_two)
    out_across = swap(chip_out, tensor_size, 2)
    d_middle, d_attn, d_shift_two, d_scale_two, d_gate_one = call(
        middle_back_kernel,
        (tokens(F32), tokens(BF16), per_latent, per_latent, per_latent),
        (
            flags,
            full_two,
            swap(full_two, tensor_size, 1),
            attn_out,
            hidden_in,
            out_cotangent,
            gate_one,
            scale_two,
        ),
        scratch=[pltpu.VMEM((tok_rows, model_width), F32)],
    )
    d_attn = after(d_attn, mlp_ring.step(d_attn))
    d_queries, d_keys, d_values, mine, theirs = call(
        attention_back_kernel,
        (features(BF16), features(BF16), features(BF16), halves, halves),
        (flags, d_attn, mixing_weight, queries, key_rows, value_rows, heads_rows),
        scratch=[pltpu.VMEM((tok_rows, model_width), F32)],
    )
    beside_one = after(swap(theirs, tensor_size, 1), mlp_ring.step(theirs))
    full_out = add(chip_out, out_across)
    chip_one = after(add(mine, beside_one), full_out)
    out_other = swap(full_out, tensor_size, 1)

    d_queries, d_keys, d_values = after((d_queries, d_keys, d_values), chip_one)
    blocks = dp_size if rings else 1
    upper_rows, lower_rows = 2 * own_feats, 2 * own_feats
    upper_part, lower_part, upper_first, lower_first, heads_bias_part = call(
        functools.partial(attention_grads_kernel, blocks),
        (
            jax.ShapeDtypeStruct((upper_rows, model_width), F32),
            jax.ShapeDtypeStruct((lower_rows, model_width), F32),
            jax.ShapeDtypeStruct((upper_rows // dp_size, model_width), F32),
            jax.ShapeDtypeStruct((lower_rows // dp_size, model_width), F32),
            jax.ShapeDtypeStruct((3, model_width), F32),
        ),
        (table, heads_in, d_queries, d_keys, d_values, attended, d_attn),
    )
    heads_ring = start_sum((upper_part, lower_part), (upper_first, lower_first), ways, dp_size, table, rings)
    block_out, d_gate_two = call(
        block_out_kernel,
        (jax.ShapeDtypeStruct((tok_rows, model_width), BF16), per_latent),
        (
            flags,
            full_out,
            after(out_other, upper_first),
            bias_rows[2],
            attn_out,
            hidden_in,
            out_cotangent,
            gate_one,
            gate_two,
        ),
        scratch=[pltpu.VMEM((tok_rows, model_width), F32)],
    )
    gate = mlp_ring.step(heads_ring.step(d_gate_two))
    across_one = after(swap(chip_one, tensor_size, 2), gate)
    full_one = add(chip_one, across_one)
    input_grad, d_shift_one, d_scale_one = call(
        input_back_kernel,
        (jax.ShapeDtypeStruct((tok_rows, model_width), F32), per_latent, per_latent),
        (
            flags,
            full_one,
            swap(full_one, tensor_size, 1),
            hidden_in,
            d_middle,
            scale_one,
        ),
        scratch=[pltpu.VMEM((tok_rows, model_width), F32)],
    )
    own_cols = modulation_weight.shape[1]
    carried = -(-(own_latents + 5) // 8) * 8
    own_mods = call(
        pack_kernel,
        jax.ShapeDtypeStruct((carried, own_cols), F32),
        (
            flags,
            d_shift_one,
            d_scale_one,
            d_gate_one,
            d_shift_two,
            d_scale_two,
            d_gate_two,
            mlp_bias,
            heads_bias_part,
        ),
        scratch=[pltpu.VMEM((own_latents, 6 * model_width), F32)],
        limit=SMALL_LIMIT,
    )
    mlp_ring.step(own_mods)
    heads_ring.step(own_mods)
    whole = (1, 1)
    run = (1, 2)
    (heads_sum, mixing_weight_sum), placed = heads_ring.finish(
        (((whole, 0),), ((run, 0), (run, 1))),
        ((3 * own_feats, model_width), (own_feats, model_width)),
    )
    (up_weight_sum, down_weight_sum), placed = mlp_ring.finish(
        (((whole, 0),), ((whole, 1),)), (up_part.shape, down_part.shape), placed
    )
    heads_weight_sum = heads_sum.reshape(3, own_feats, model_width).transpose(2, 0, 1)
    all_mods = gather_latents(own_mods, dp_size)
    mod_weight_sum, mod_bias_row, d_silu_part, bias_sum = call(
        functools.partial(modulation_grad_kernel, own_latents),
        (
            jax.ShapeDtypeStruct((model_width, own_cols), F32),
            jax.ShapeDtypeStruct((1, own_cols), F32),
            jax.ShapeDtypeStruct((silu_all.shape[0], model_width), F32),
            jax.ShapeDtypeStruct((5, own_cols), F32),
        ),
        (all_mods, silu_all, modulation_weight),
        scalars=0,
    )
    mod_bias_sum = mod_bias_row.reshape(own_cols)
    up_bias_sum, down_bias_sum, mixing_bias_sum = (bias_sum[row, :model_width] for row in range(3))
    heads_bias_sum = bias_sum[3:5, :own_feats]
    d_silu_own = scatter_features(d_silu_part, tensor_size)
    sigmoid_part = jax.nn.sigmoid(cond_part)
    d_condition = d_silu_own * sigmoid_part * (1.0 + cond_part * (1.0 - sigmoid_part))
    exact = dict(preferred_element_type=F32, precision=lax.Precision.HIGHEST)
    class_sum = jnp.einsum("lk,lf->kf", class_pick.astype(F32), d_condition, **exact)
    time_sum = jnp.einsum("lk,lf->kf", time_pick.astype(F32), d_condition, **exact)
    return (
        block_out,
        input_grad,
        mod_weight_sum,
        mod_bias_sum,
        heads_weight_sum,
        heads_bias_sum,
        mixing_weight_sum,
        mixing_bias_sum,
        up_weight_sum,
        up_bias_sum,
        down_weight_sum,
        down_bias_sum,
        class_sum,
        time_sum,
    )


def solution(mesh):
    in_specs = (
        P("dp", None),
        P("dp", None),
        P(),
        P(),
        P(None, "tensor"),
        P("tensor"),
        P(None, None, "tensor"),
        P(None, "tensor"),
        P("tensor", None),
        P(),
        P(None, "tensor"),
        P("tensor"),
        P("tensor", None),
        P(),
        P(None, "tensor"),
        P(None, "tensor"),
    )
    out_specs = (
        P("dp", None),
        P("dp", None),
        P(None, "tensor"),
        P("tensor"),
        P(None, None, "tensor"),
        P(None, "tensor"),
        P("tensor", None),
        P(),
        P(None, "tensor"),
        P("tensor"),
        P("tensor", None),
        P(),
        P(None, "tensor"),
        P(None, "tensor"),
    )

    def run(*args):
        return on_device(mesh.shape["tensor"], mesh.shape["dp"], *args)

    return jax.shard_map(run, mesh=mesh, in_specs=in_specs, out_specs=out_specs, check_vma=False)
```
